512 devices in a mesh: stream: 16 (over z, x_hi), span: 32 (over y, x_lo, core).
Axes of the slice: x: 4 (x_hi: 2, x_lo: 2; x = x_hi * 2 + x_lo), y: 8, z: 8, core: 2. Of those that a mesh axis runs over, the one named last changes fastest.
Arguments:
- pre_pops: float32 [19, 128, 256, 128], P(None, 'stream', 'span'), may hold values from 0.7 to 1.3
- main_pops: float32 [19, 128, 256, 256], P(None, 'stream', 'span'), may hold values from 0.7 to 1.3
- tile_map: int32 [32], replicated, may hold values from 0 to 31, each once
- layer_phase: int32 [32], replicated, may hold values from 0 to 1
- wall_flags: int32 [256], replicated, may hold values 0 or 1
Outputs:
- pre_out: float32 [19, 128, 256, 128], P(None, 'stream', 'span')
- main_out: float32 [19, 128, 256, 256], P(None, 'stream', 'span')
The draws below stay inside these ranges and needn't reach their ends.
Inputs may be any that keep to these rules, and one draw needn't show every extreme that they name: `tile_map`: each precursor tile feeds exactly one inlet tile.
All inputs are finite; a program needn't handle non-finite values.
Results may differ from the reference program's by a relative error of at most 0.0003.
Values sent between devices are 32-bit elements; how exact they have to be, the bound alone decides.
A program may use at most 64 MiB of HBM per device.

```python
import jax
import jax.numpy as jnp
from jax import lax

CX = 8
NW = 256
STEPS = 2
NWC = 128
NX = 128
NZ = 256
SPAN_TILES = 32


def place_ends(drawn, stream_key, least, top_value):
    index_at = [jax.random.randint(jax.random.fold_in(stream_key, axis), (), 0, length) for axis, length in enumerate(drawn.shape)]
    main_axis = drawn.shape.index(max(drawn.shape))
    next_to = index_at[:main_axis] + [(index_at[main_axis] + 1) % drawn.shape[main_axis]] + index_at[main_axis + 1:]
    return drawn.at[tuple(index_at)].set(least).at[tuple(next_to)].set(top_value)


def levels(rng, shape, pieces, least, top_value):
    gain = 1.0
    for axis_at, blocks in pieces:
        steps = jax.random.uniform(jax.random.fold_in(jax.random.fold_in(rng, 6), axis_at), (blocks,), jnp.float32, least / len(pieces), top_value / len(pieces))
        gain = gain * jnp.repeat(jnp.exp(steps), shape[axis_at] // blocks).reshape((-1,) + (1,) * (len(shape) - 1 - axis_at))
    return gain


def setup_inputs(seed: int = 0) -> dict:
    keys = jax.random.split(jax.random.key(seed), 6)
    return {
        "pre_pops": jnp.clip(0.7 + 0.59999996 * jax.random.uniform(keys[0], (19, NX, NZ, NWC), jnp.float32) ** levels(keys[0], (19, NX, NZ, NWC), ((1, 16), (2, 32)), -0.2, 0.2), 0.7, 1.3),
        "main_pops": jnp.clip(0.7 + 0.59999996 * jax.random.uniform(keys[1], (19, NX, NZ, NW), jnp.float32) ** levels(keys[1], (19, NX, NZ, NW), ((1, 16), (2, 32)), -0.2, 0.2), 0.7, 1.3),
        "tile_map": jax.random.permutation(keys[2], SPAN_TILES).astype(jnp.int32),
        "layer_phase": place_ends(jax.random.randint(keys[3], (SPAN_TILES,), 0, 2), jax.random.fold_in(keys[3], 1), 0, 1).astype(jnp.int32),
        "wall_flags": place_ends((jax.random.randint(keys[4], (NW,), 0, 8) < 1).astype(jnp.int32), jax.random.fold_in(keys[4], 1), 0, 1),
    }


velocities = ((0, 0, 0), (1, 0, 0), (-1, 0, 0), (0, 1, 0), (0, -1, 0), (0, 0, 1), (0, 0, -1), (1, 1, 0), (-1, -1, 0), (1, -1, 0), (-1, 1, 0), (1, 0, 1), (-1, 0, -1), (1, 0, -1), (-1, 0, 1), (0, 1, 1), (0, -1, -1), (0, 1, -1), (0, -1, 1))
opposite = (0, 2, 1, 4, 3, 6, 5, 8, 7, 10, 9, 12, 11, 14, 13, 16, 15, 18, 17)
lattice_weights = (1.0 / 3.0,) + (1.0 / 18.0,) * 6 + (1.0 / 36.0,) * 12
incoming = (1, 7, 9, 11, 13)
relax_rate = 1.25


def collide(pops):
    density = jnp.zeros_like(pops[0])
    moment = [jnp.zeros_like(pops[0]) for axis_num in range(3)]
    for which_pop in range(19):
        weighted = lattice_weights[which_pop] * pops[which_pop]
        density = density + weighted
        for axis_num in range(3):
            if velocities[which_pop][axis_num] != 0:
                moment[axis_num] = moment[axis_num] + velocities[which_pop][axis_num] * weighted
    speed = [component / density for component in moment]
    square = speed[0] * speed[0] + speed[1] * speed[1] + speed[2] * speed[2]
    result = []
    for which_pop in range(19):
        projected = jnp.zeros_like(density)
        for axis_num in range(3):
            if velocities[which_pop][axis_num] != 0:
                projected = projected + velocities[which_pop][axis_num] * speed[axis_num]
        balance = density * (1.0 + 3.0 * projected + 4.5 * projected * projected - 1.5 * square)
        result.append(pops[which_pop] - relax_rate * (pops[which_pop] - balance))
    return jnp.stack(result)


def stream(padded, collided, solid):
    row_len = collided.shape[1]
    span_len = collided.shape[2]
    layers = collided.shape[3]
    walled = jnp.concatenate([jnp.ones((1,), jnp.int32), solid.astype(jnp.int32), jnp.ones((1,), jnp.int32)])
    result = []
    for which_pop in range(19):
        step_x, step_y, step_z = velocities[which_pop]
        source = padded[which_pop, 1 - step_x:1 - step_x + row_len, 1 - step_z:1 - step_z + span_len, :]
        if step_y == 1:
            source = jnp.concatenate([jnp.zeros_like(source[..., :1]), source[..., :-1]], axis=-1)
        elif step_y == -1:
            source = jnp.concatenate([source[..., 1:], jnp.zeros_like(source[..., :1])], axis=-1)
        blocked = walled[1 - step_y:1 - step_y + layers] > 0
        result.append(jnp.where(blocked, collided[opposite[which_pop]], source))
    return jnp.stack(result)


def spread_matrix(coarse_len, fine_len, tile_phase):
    fine_pos = jnp.arange(fine_len, dtype=jnp.int32) + tile_phase.astype(jnp.int32)
    lower = (fine_pos - 1) // 2
    upper_wt = jnp.where(fine_pos % 2 == 0, 0.75, 0.25).astype(jnp.float32)
    low_idx = jnp.clip(lower, 0, coarse_len - 1)
    high_idx = jnp.clip(lower + 1, 0, coarse_len - 1)
    coarse_rows = jnp.arange(coarse_len, dtype=jnp.int32)[:, None]
    return jnp.where(coarse_rows == low_idx[None, :], 1.0 - upper_wt[None, :], 0.0).astype(jnp.float32) + jnp.where(coarse_rows == high_idx[None, :], upper_wt[None, :], 0.0).astype(jnp.float32)


def refine(coarse, tile_phase, fine_len):
    matrix = spread_matrix(coarse.shape[-1], fine_len, tile_phase)
    return jnp.dot(coarse, matrix, precision=lax.Precision.HIGHEST, preferred_element_type=jnp.float32)


def reference(pre_pops, main_pops, tile_map, layer_phase, wall_flags):
    coarse_len = pre_pops.shape[3]
    fine_len = main_pops.shape[3]
    solid_coarse = jnp.max(wall_flags.reshape(coarse_len, 2), axis=1)
    tile_count = tile_map.shape[0]
    tile_width = main_pops.shape[2] // tile_count
    for step_num in range(STEPS):
        pre_star = collide(pre_pops)
        main_star = collide(main_pops)
        pre_pad = jnp.pad(pre_star, ((0, 0), (1, 1), (1, 1), (0, 0)), mode="wrap")
        outflow = jnp.stack([pre_star[which_pop, CX - 1] for which_pop in incoming])
        blocks = outflow.reshape(5, tile_count, tile_width, coarse_len).transpose(1, 0, 2, 3)
        chosen = blocks[tile_map]
        fine_blocks = jax.vmap(lambda chosen_block, tile_phase: refine(chosen_block, tile_phase, fine_len))(chosen, layer_phase)
        inflow = fine_blocks.transpose(1, 0, 2, 3).reshape(5, tile_count * tile_width, fine_len)
        inflow = jnp.pad(inflow, ((0, 0), (1, 1), (0, 0)), mode="wrap")
        span_padded = jnp.pad(main_star, ((0, 0), (0, 0), (1, 1), (0, 0)), mode="wrap")
        ghost_plane = jnp.zeros_like(span_padded[:, 0])
        ghost_plane = ghost_plane.at[jnp.array(incoming, dtype=jnp.int32)].set(inflow)
        main_pad = jnp.concatenate([ghost_plane[:, None], span_padded, span_padded[:, -1:]], axis=1)
        pre_pops = stream(pre_pad, pre_star, solid_coarse)
        main_pops = stream(main_pad, main_star, wall_flags)
    return pre_pops, main_pops
```

```python
import jax
import jax.numpy as jnp
from jax import lax
from jax.experimental import pallas as pl
from jax.experimental.pallas import tpu as pltpu

VELOCITIES = (
    (0, 0, 0),
    (1, 0, 0), (-1, 0, 0), (0, 1, 0), (0, -1, 0), (0, 0, 1), (0, 0, -1),
    (1, 1, 0), (-1, -1, 0), (1, -1, 0), (-1, 1, 0),
    (1, 0, 1), (-1, 0, -1), (1, 0, -1), (-1, 0, 1),
    (0, 1, 1), (0, -1, -1), (0, 1, -1), (0, -1, 1),
)
OPPOSITE = (0, 2, 1, 4, 3, 6, 5, 8, 7, 10, 9, 12, 11, 14, 13, 16, 15, 18, 17)
ORDER = (1, 7, 9, 11, 13, 2, 8, 10, 12, 14, 0, 3, 4, 5, 6, 15, 16, 17, 18)
POS = tuple(ORDER.index(i) for i in range(19))
Z_UP = (5, 11, 14, 15, 18)
Z_DOWN = (6, 12, 13, 16, 17)
PAIRS = ((1, 2), (3, 4), (5, 6), (7, 8), (9, 10), (11, 12), (13, 14), (15, 16), (17, 18))
CX, CZ = 8, 8
NP, NM = 128, 256
LANES = NP + NM
STREAM, SPAN = 16, 32
ROWS, COLS = 8, 4
MESH = pl.DeviceIdType.MESH


def collide_planes(load, store, x):
    for lane in range(3):
        g = [load(i, x, lane) for i in range(19)]
        diff = {a: g[a] - g[b] for a, b in PAIRS}
        both = {a: g[a] + g[b] for a, b in PAIRS}
        axes = both[1] + both[3] + both[5]
        edges = (both[7] + both[9]) + (both[11] + both[13]) + (both[15] + both[17])
        density = (1.0 / 3.0) * g[0] + (1.0 / 18.0) * axes + (1.0 / 36.0) * edges
        mx = (1.0 / 18.0) * diff[1] + (1.0 / 36.0) * ((diff[7] + diff[9]) + (diff[11] + diff[13]))
        my = (1.0 / 18.0) * diff[3] + (1.0 / 36.0) * ((diff[7] - diff[9]) + (diff[15] + diff[17]))
        mz = (1.0 / 18.0) * diff[5] + (1.0 / 36.0) * ((diff[11] - diff[13]) + (diff[15] - diff[17]))
        inverse = 1.0 / density
        base = 1.25 * density - (1.875 * inverse) * (mx * mx + my * my + mz * mz)
        scale = 5.625 * inverse
        store(0, x, lane, base - 0.25 * g[0])
        moment = (mx, my, mz)
        for a, b in PAIRS:
            along = None
            for axis in range(3):
                c = VELOCITIES[a][axis]
                if c:
                    term = moment[axis]
                    if along is None:
                        along = term
                    else:
                        along = along + term if c > 0 else along - term
            even = base + scale * (along * along)
            odd = 3.75 * along
            store(a, x, lane, (even + odd) - 0.25 * g[a])
            store(b, x, lane, (even - odd) - 0.25 * g[b])


def body(tile_ref, phase_ref, wall_ref, pre_ref, main_ref, pre_out, main_out,
         star, zsend, zrecv, temp, masks, spread, rows_a, rows_b, pay_send, pay_a, pay_b,
         xs_sem, xr_sem, zs_sem, zr_sem, cs_sem, cr_sem, ys_sem, yr_sem, qs_sem, qr_sem):
    rows_buf, pay_recv = (rows_a, rows_b), (pay_a, pay_b)
    st = lax.axis_index("stream")
    sp = lax.axis_index("span")
    st_up, st_down = lax.rem(st + 1, STREAM), lax.rem(st + STREAM - 1, STREAM)
    sp_up, sp_down = lax.rem(sp + 1, SPAN), lax.rem(sp + SPAN - 1, SPAN)
    row, col = lax.div(sp, COLS), lax.rem(sp, COLS)

    barrier = pltpu.get_barrier_semaphore()
    for a in (st_up, st, st_down):
        for b in (sp_up, sp, sp_down):
            if a is st and b is sp:
                continue
            pl.semaphore_signal(barrier, inc=1, device_id=(a, b), device_id_type=MESH)

    @pl.when(st == 0)
    def _():
        for d in range(1, ROWS):
            peer = lax.rem(row + d, ROWS) * COLS + col
            pl.semaphore_signal(barrier, inc=1, device_id=(st, peer), device_id_type=MESH)
        for e in range(1, COLS):
            peer = row * COLS + lax.rem(col + e, COLS)
            pl.semaphore_signal(barrier, inc=1, device_id=(st, peer), device_id_type=MESH)

    def remote(src, dst, send, recv, device):
        return pltpu.make_async_remote_copy(
            src_ref=src, dst_ref=dst, send_sem=send, recv_sem=recv,
            device_id=device, device_id_type=MESH)

    def x_copy(step, way):
        if way == 0:
            return remote(star.at[step, 0:5, CX], star.at[step, 0:5, 0],
                          xs_sem.at[step, 0], xr_sem.at[step, 0], (st_up, sp))
        return remote(star.at[step, 5:10, 1], star.at[step, 5:10, CX + 1],
                      xs_sem.at[step, 1], xr_sem.at[step, 1], (st_down, sp))

    def z_copy(step, way):
        return remote(zsend.at[step, way], zrecv.at[step, way, :, 1:CX + 1],
                      zs_sem.at[step, way], zr_sem.at[step, way],
                      (st, sp_up if way == 0 else sp_down))

    def corner_copy(step, which):
        way, pop, x, slot, device = (
            (0, Z_UP.index(11), CX - 1, 0, (st_up, sp_up)),
            (0, Z_UP.index(14), 0, CX + 1, (st_down, sp_up)),
            (1, Z_DOWN.index(12), 0, CX + 1, (st_down, sp_down)),
            (1, Z_DOWN.index(13), CX - 1, 0, (st_up, sp_down)),
        )[which]
        return remote(zsend.at[step, way, pop, x], zrecv.at[step, way, pop, slot],
                      cs_sem.at[step, which], cr_sem.at[step, which], device)

    def row_copy(step, d):
        peer = lax.rem(row + d, ROWS) * COLS + col
        return remote(star.at[step, 0:5, CX, :, 0:NP], rows_buf[step].at[d],
                      ys_sem.at[step, d], yr_sem.at[step, d], (st, peer))

    def quad_copy(step, e):
        peer = row * COLS + lax.rem(col + e, COLS)
        return remote(pay_send.at[step, e], pay_recv[step].at[e],
                      qs_sem.at[step, e], qr_sem.at[step, e], (st, peer))

    def lanes(lane):
        return slice(lane * 128, lane * 128 + 128)

    def load_input(i, x, lane):
        if lane == 0:
            return pre_ref[i, x]
        return main_ref[i, x, :, lanes(lane - 1)]

    def load_temp(i, x, lane):
        return temp[i, :, lanes(lane)]

    def store_star(step):
        def store(i, x, lane, value):
            star[step, POS[i], x + 1, :, lanes(lane)] = value
            if i in Z_UP:
                zsend[step, 0, Z_UP.index(i), x, :, lanes(lane)] = value[CZ - 1:CZ, :]
            if i in Z_DOWN:
                zsend[step, 1, Z_DOWN.index(i), x, :, lanes(lane)] = value[0:1, :]
        return store

    row_id = lax.broadcasted_iota(jnp.int32, (CZ, LANES), 0)

    def stream_plane(step, x, write):
        for i in range(19):
            cx, cy, cz = VELOCITIES[i]
            source = star[step, POS[i], x + 1 - cx]
            if cz == 1:
                edge = zrecv[step, 0, Z_UP.index(i), x + 1 - cx]
                source = jnp.where(row_id == 0, jnp.broadcast_to(edge, (CZ, LANES)),
                                   pltpu.roll(source, 1, 0))
            elif cz == -1:
                edge = zrecv[step, 1, Z_DOWN.index(i), x + 1 - cx]
                source = jnp.where(row_id == CZ - 1, jnp.broadcast_to(edge, (CZ, LANES)),
                                   pltpu.roll(source, CZ - 1, 0))
            if cy == 1:
                source = pltpu.roll(source, 1, 1)
            elif cy == -1:
                source = pltpu.roll(source, LANES - 1, 1)
            write(i, jnp.where(masks[cy % 3] > 0.5, star[step, POS[OPPOSITE[i]], x + 1], source))

    def write_temp(i, value):
        temp[i] = value

    def advance(x):
        stream_plane(0, x, write_temp)
        collide_planes(load_temp, store_star(1), x)

    def finish(x):
        def write(i, value):
            pre_out[i, x] = value[:, 0:NP]
            main_out[i, x] = value[:, NP:]
        stream_plane(1, x, write)

    def rows_start(step):
        @pl.when(st == 0)
        def _():
            for d in range(1, ROWS):
                row_copy(step, d).start()
            rows_buf[step][0] = star[step, 0:5, CX, :, 0:NP]

    small_row = lax.broadcasted_iota(jnp.int32, (CZ, 128), 0)

    def row_slot(tile):
        return lax.rem(row - lax.div(tile, COLS) + ROWS, ROWS)

    def col_slot(tile):
        return lax.rem(col - lax.rem(tile, COLS) + COLS, COLS)

    def quads_start(step):
        @pl.when(st == 0)
        def _():
            for d in range(1, ROWS):
                row_copy(step, d).wait()
            for e in range(COLS):
                target = row * COLS + lax.rem(col + e, COLS)
                own = tile_ref[target]
                left = tile_ref[lax.rem(target + SPAN - 1, SPAN)]
                right = tile_ref[lax.rem(target + 1, SPAN)]
                out = pay_recv[step].at[0] if e == 0 else pay_send.at[step, e]
                out[0:5] = rows_buf[step][row_slot(own)]
                out[5] = jnp.where(
                    small_row == 0,
                    pltpu.roll(rows_buf[step][row_slot(left), 3], 1, 0),
                    pltpu.roll(rows_buf[step][row_slot(right), 4], 1, 0))
                if e:
                    quad_copy(step, e).start()

    def inlet(step):
        @pl.when(st == 0)
        def _():
            for e in range(1, COLS):
                quad_copy(step, e).wait()
            left_at = lax.rem(sp + SPAN - 1, SPAN)
            right_at = lax.rem(sp + 1, SPAN)
            tile = pay_recv[step][col_slot(tile_ref[sp]), 0:5]
            edge = jnp.where(small_row == 0,
                             pay_recv[step][col_slot(tile_ref[left_at]), 5],
                             pay_recv[step][col_slot(tile_ref[right_at]), 5])
            coarse = jnp.concatenate([tile.reshape(5 * CZ, 128), edge], axis=0)
            fine = jnp.dot(coarse, spread[...], precision=lax.Precision.HIGHEST,
                           preferred_element_type=jnp.float32)
            own_phase = jnp.full((5 * CZ, NM), phase_ref[sp], jnp.int32)
            plane = jnp.where(own_phase == 0, fine[0:5 * CZ, 0:NM], fine[0:5 * CZ, NM:])
            plane = plane.reshape(5, CZ, NM)
            for k in range(5):
                star[step, k, 0, :, NP:] = plane[k]
            tail = fine[5 * CZ:, :]
            left_phase = jnp.full((CZ, NM), phase_ref[left_at], jnp.int32)
            right_phase = jnp.full((CZ, NM), phase_ref[right_at], jnp.int32)
            left = jnp.where(left_phase == 0, tail[:, 0:NM], tail[:, NM:])
            right = jnp.where(right_phase == 0, tail[:, 0:NM], tail[:, NM:])
            zrecv[step, 0, Z_UP.index(11), 0, :, NP:] = left[0:1]
            zrecv[step, 1, Z_DOWN.index(13), 0, :, NP:] = right[1:2]

    def outlet(step):
        @pl.when(st == STREAM - 1)
        def _():
            for k in range(5, 10):
                star[step, k, CX + 1, :, NP:] = star[step, k, CX, :, NP:]
            for way, pop in ((0, Z_UP.index(14)), (1, Z_DOWN.index(12))):
                zrecv[step, way, pop, CX + 1, :, NP:] = zrecv[step, way, pop, CX, :, NP:]

    collide_planes(load_input, store_star(0), CX - 1)

    @pl.when(st == 0)
    def _():
        pl.semaphore_wait(barrier, 8 + ROWS + COLS - 2)

    @pl.when(st != 0)
    def _():
        pl.semaphore_wait(barrier, 8)

    x_copy(0, 0).start()
    rows_start(0)
    collide_planes(load_input, store_star(0), 0)
    x_copy(0, 1).start()

    def first(x, carry):
        collide_planes(load_input, store_star(0), x)
        return carry

    lax.fori_loop(1, CX - 1, first, 0)
    for way in range(2):
        z_copy(0, way).start()
    for which in range(4):
        corner_copy(0, which).start()

    wall = jnp.broadcast_to(wall_ref[...].astype(jnp.float32), (CZ, NM))
    fine_id = lax.broadcasted_iota(jnp.int32, (NM, NP), 0)
    coarse_id = lax.broadcasted_iota(jnp.int32, (NM, NP), 1)
    pick = jnp.where(lax.shift_right_logical(fine_id, 1) == coarse_id, 1.0, 0.0)
    merged = jnp.dot(wall, pick, preferred_element_type=jnp.float32)
    coarse_wall = jnp.where(merged > 0.5, 1.0, 0.0)
    solid = jnp.concatenate([coarse_wall, wall], axis=1)
    lane_id = lax.broadcasted_iota(jnp.int32, (CZ, LANES), 1)
    masks[0] = solid
    masks[1] = jnp.where((lane_id == 0) | (lane_id == NP), 1.0, pltpu.roll(solid, 1, 1))
    masks[2] = jnp.where((lane_id == NP - 1) | (lane_id == LANES - 1), 1.0,
                         pltpu.roll(solid, LANES - 1, 1))

    @pl.when(st == 0)
    def _():
        coarse_row = lax.broadcasted_iota(jnp.int32, (NP, NM), 0)
        fine_col = lax.broadcasted_iota(jnp.int32, (NP, NM), 1)
        for phase in range(2):
            place = fine_col + phase
            lower = lax.shift_right_arithmetic(place - 1, 1)
            upper = jnp.where((place & 1) == 0, 0.75, 0.25)
            low = jnp.clip(lower, 0, NP - 1)
            high = jnp.clip(lower + 1, 0, NP - 1)
            spread[:, phase * NM:(phase + 1) * NM] = (
                jnp.where(coarse_row == low, 1.0 - upper, 0.0)
                + jnp.where(coarse_row == high, upper, 0.0))

    for step in range(2):
        plane = advance if step == 0 else finish

        def inner(x, carry):
            plane(x)
            return carry

        for way in range(2):
            z_copy(step, way).wait()
        lax.fori_loop(1, CX - 1, inner, 0)
        quads_start(step)
        for way in range(2):
            x_copy(step, way).wait()
        for which in range(4):
            corner_copy(step, which).wait()
        outlet(step)
        plane(CX - 1)
        if step == 0:
            x_copy(1, 0).start()
            rows_start(1)
        inlet(step)
        plane(0)
        if step == 0:
            x_copy(1, 1).start()
            for way in range(2):
                z_copy(1, way).start()
            for which in range(4):
                corner_copy(1, which).start()


def local(pre_pops, main_pops, tile_map, layer_phase, wall_flags):
    vmem = pl.BlockSpec(memory_space=pltpu.VMEM)
    smem = pl.BlockSpec(memory_space=pltpu.SMEM)
    dma = pltpu.SemaphoreType.DMA
    f32 = jnp.float32
    return pl.pallas_call(
        body,
        out_shape=(jax.ShapeDtypeStruct(pre_pops.shape, f32),
                   jax.ShapeDtypeStruct(main_pops.shape, f32)),
        in_specs=[smem, smem, vmem, vmem, vmem],
        out_specs=(vmem, vmem),
        scratch_shapes=[
            pltpu.VMEM((2, 19, CX + 2, CZ, LANES), f32),
            pltpu.VMEM((2, 2, 5, CX, 1, LANES), f32),
            pltpu.VMEM((2, 2, 5, CX + 2, 1, LANES), f32),
            pltpu.VMEM((19, CZ, LANES), f32),
            pltpu.VMEM((3, CZ, LANES), f32),
            pltpu.VMEM((NP, 2 * NM), f32),
            pltpu.VMEM((ROWS, 5, CZ, NP), f32),
            pltpu.VMEM((ROWS, 5, CZ, NP), f32),
            pltpu.VMEM((2, COLS, 6, CZ, NP), f32),
            pltpu.VMEM((COLS, 6, CZ, NP), f32),
            pltpu.VMEM((COLS, 6, CZ, NP), f32),
            dma((2, 2)), dma((2, 2)), dma((2, 2)), dma((2, 2)),
            dma((2, 4)), dma((2, 4)),
            dma((2, ROWS)), dma((2, ROWS)), dma((2, COLS)), dma((2, COLS)),
        ],
        compiler_params=pltpu.CompilerParams(
            collective_id=0, has_side_effects=True, vmem_limit_bytes=60 * 1024 * 1024),
    )(tile_map, layer_phase, wall_flags.reshape(1, NM), pre_pops, main_pops)


def solution(mesh):
    spec = jax.sharding.PartitionSpec
    blocks = spec(None, "stream", "span", None)
    return jax.shard_map(
        local,
        mesh=mesh,
        in_specs=(blocks, blocks, spec(), spec(), spec()),
        out_specs=(blocks, blocks),
        check_vma=False,
    )
```

```python
import jax
import jax.numpy as jnp
from jax import lax
from jax.experimental import pallas as pl
from jax.experimental.pallas import tpu as pltpu

VELOCITIES = (
    (0, 0, 0),
    (1, 0, 0), (-1, 0, 0), (0, 1, 0), (0, -1, 0), (0, 0, 1), (0, 0, -1),
    (1, 1, 0), (-1, -1, 0), (1, -1, 0), (-1, 1, 0),
    (1, 0, 1), (-1, 0, -1), (1, 0, -1), (-1, 0, 1),
    (0, 1, 1), (0, -1, -1), (0, 1, -1), (0, -1, 1),
)
OPPOSITE = (0, 2, 1, 4, 3, 6, 5, 8, 7, 10, 9, 12, 11, 14, 13, 16, 15, 18, 17)
ORDER = (1, 7, 9, 11, 13, 2, 8, 10, 12, 14, 0, 3, 4, 5, 6, 15, 16, 17, 18)
POS = tuple(ORDER.index(i) for i in range(19))
Z_UP = (5, 11, 14, 15, 18)
Z_DOWN = (6, 12, 13, 16, 17)
PAIRS = ((1, 2), (3, 4), (5, 6), (7, 8), (9, 10), (11, 12), (13, 14), (15, 16), (17, 18))
CX, CZ = 8, 8
NP, NM = 128, 256
LANES = NP + NM
STREAM, SPAN = 16, 32
ROWS, COLS = 8, 4
MESH = pl.DeviceIdType.MESH


def collide_planes(load, store, x, chunks=(0, 1, 2)):
    for lane in chunks:
        g = [load(i, x, lane) for i in range(19)]
        diff = {a: g[a] - g[b] for a, b in PAIRS}
        both = {a: g[a] + g[b] for a, b in PAIRS}
        axes = both[1] + both[3] + both[5]
        edges = (both[7] + both[9]) + (both[11] + both[13]) + (both[15] + both[17])
        density = (1.0 / 3.0) * g[0] + (1.0 / 18.0) * axes + (1.0 / 36.0) * edges
        mx = (1.0 / 18.0) * diff[1] + (1.0 / 36.0) * ((diff[7] + diff[9]) + (diff[11] + diff[13]))
        my = (1.0 / 18.0) * diff[3] + (1.0 / 36.0) * ((diff[7] - diff[9]) + (diff[15] + diff[17]))
        mz = (1.0 / 18.0) * diff[5] + (1.0 / 36.0) * ((diff[11] - diff[13]) + (diff[15] - diff[17]))
        inverse = 1.0 / density
        base = 1.25 * density - (1.875 * inverse) * (mx * mx + my * my + mz * mz)
        scale = 5.625 * inverse
        store(0, x, lane, base - 0.25 * g[0])
        moment = (mx, my, mz)
        for a, b in PAIRS:
            along = None
            for axis in range(3):
                c = VELOCITIES[a][axis]
                if c:
                    term = moment[axis]
                    if along is None:
                        along = term
                    else:
                        along = along + term if c > 0 else along - term
            even = base + scale * (along * along)
            odd = 3.75 * along
            store(a, x, lane, (even + odd) - 0.25 * g[a])
            store(b, x, lane, (even - odd) - 0.25 * g[b])


def body(tile_hbm, phase_hbm, wall_hbm, pre_hbm, main_hbm, pre_out, main_out,
         tile_ref, phase_ref, wall_ref, pre_ref, main_ref, star, zsend, zrecv, temp, masks, spread, rows_a, rows_b, pay_send, pay_a, pay_b,
         xs_sem, xr_sem, zs_sem, zr_sem, cs_sem, cr_sem, ys_sem, yr_sem, qs_sem, qr_sem, in_sem):
    rows_buf, pay_recv = (rows_a, rows_b), (pay_a, pay_b)
    st = lax.axis_index("stream")
    sp = lax.axis_index("span")
    st_up, st_down = lax.rem(st + 1, STREAM), lax.rem(st + STREAM - 1, STREAM)
    sp_up, sp_down = lax.rem(sp + 1, SPAN), lax.rem(sp + SPAN - 1, SPAN)
    row, col = lax.div(sp, COLS), lax.rem(sp, COLS)

    barrier = pltpu.get_barrier_semaphore()
    for a in (st_up, st, st_down):
        for b in (sp_up, sp, sp_down):
            if a is st and b is sp:
                continue
            pl.semaphore_signal(barrier, inc=1, device_id=(a, b), device_id_type=MESH)

    @pl.when(st == 0)
    def _():
        for d in range(1, ROWS):
            peer = lax.rem(row + d, ROWS) * COLS + col
            pl.semaphore_signal(barrier, inc=1, device_id=(st, peer), device_id_type=MESH)
        for e in range(1, COLS):
            peer = row * COLS + lax.rem(col + e, COLS)
            pl.semaphore_signal(barrier, inc=1, device_id=(st, peer), device_id_type=MESH)

    loads = [pltpu.make_async_copy(source, target, in_sem.at[at])
             for at, (source, target) in enumerate((
                 (pre_hbm, pre_ref), (main_hbm, main_ref), (wall_hbm, wall_ref),
                 (tile_hbm, tile_ref), (phase_hbm, phase_ref)))]
    for load in loads:
        load.start()

    def remote(src, dst, send, recv, device):
        return pltpu.make_async_remote_copy(
            src_ref=src, dst_ref=dst, send_sem=send, recv_sem=recv,
            device_id=device, device_id_type=MESH)

    PRE, MAIN = slice(0, NP), slice(NP, LANES)

    def x_copy(step, way, part):
        cut = (PRE, MAIN)[part]
        if way == 0:
            return remote(star.at[step, 0:5, CX, :, cut], star.at[step, 0:5, 0, :, cut],
                          xs_sem.at[step, 0, part], xr_sem.at[step, 0, part], (st_up, sp))
        return remote(star.at[step, 5:10, 1, :, cut], star.at[step, 5:10, CX + 1, :, cut],
                      xs_sem.at[step, 1, part], xr_sem.at[step, 1, part], (st_down, sp))

    def z_copy(step, way):
        return remote(zsend.at[step, way], zrecv.at[step, way, :, 1:CX + 1],
                      zs_sem.at[step, way], zr_sem.at[step, way],
                      (st, sp_up if way == 0 else sp_down))

    def corner_copy(step, which):
        way, pop, x, slot, device = (
            (0, Z_UP.index(11), CX - 1, 0, (st_up, sp_up)),
            (0, Z_UP.index(14), 0, CX + 1, (st_down, sp_up)),
            (1, Z_DOWN.index(12), 0, CX + 1, (st_down, sp_down)),
            (1, Z_DOWN.index(13), CX - 1, 0, (st_up, sp_down)),
        )[which]
        return remote(zsend.at[step, way, pop, x], zrecv.at[step, way, pop, slot],
                      cs_sem.at[step, which], cr_sem.at[step, which], device)

    def row_copy(step, d):
        peer = lax.rem(row + d, ROWS) * COLS + col
        return remote(star.at[step, 0:5, CX, :, 0:NP], rows_buf[step].at[d],
                      ys_sem.at[step, d], yr_sem.at[step, d], (st, peer))

    def quad_copy(step, e):
        peer = row * COLS + lax.rem(col + e, COLS)
        return remote(pay_send.at[step, e], pay_recv[step].at[e],
                      qs_sem.at[step, e], qr_sem.at[step, e], (st, peer))

    def lanes(lane):
        return slice(lane * 128, lane * 128 + 128)

    def load_input(i, x, lane):
        if lane == 0:
            return pre_ref[i, x]
        return main_ref[i, x, :, lanes(lane - 1)]

    def load_temp(i, x, lane):
        return temp[i, :, lanes(lane)]

    def store_star(step):
        def store(i, x, lane, value):
            star[step, POS[i], x + 1, :, lanes(lane)] = value
            if i in Z_UP:
                zsend[step, 0, Z_UP.index(i), x, :, lanes(lane)] = value[CZ - 1:CZ, :]
            if i in Z_DOWN:
                zsend[step, 1, Z_DOWN.index(i), x, :, lanes(lane)] = value[0:1, :]
        return store

    def stream_plane(step, x, cut, write):
        width = cut.stop - cut.start
        row_id = lax.broadcasted_iota(jnp.int32, (CZ, width), 0)
        for i in range(19):
            cx, cy, cz = VELOCITIES[i]
            source = star[step, POS[i], x + 1 - cx, :, cut]
            if cz == 1:
                edge = zrecv[step, 0, Z_UP.index(i), x + 1 - cx, :, cut]
                source = jnp.where(row_id == 0, jnp.broadcast_to(edge, (CZ, width)),
                                   pltpu.roll(source, 1, 0))
            elif cz == -1:
                edge = zrecv[step, 1, Z_DOWN.index(i), x + 1 - cx, :, cut]
                source = jnp.where(row_id == CZ - 1, jnp.broadcast_to(edge, (CZ, width)),
                                   pltpu.roll(source, CZ - 1, 0))
            if cy == 1:
                source = pltpu.roll(source, 1, 1)
            elif cy == -1:
                source = pltpu.roll(source, width - 1, 1)
            bounced = star[step, POS[OPPOSITE[i]], x + 1, :, cut]
            write(i, jnp.where(masks[cy % 3, :, cut] > 0.5, bounced, source))

    def advance(x, cut=slice(0, LANES)):
        def write(i, value):
            temp[i, :, cut] = value
        stream_plane(0, x, cut, write)
        collide_planes(load_temp, store_star(1), x, range(cut.start // 128, cut.stop // 128))

    def finish(x):
        def write(i, value):
            pre_out[i, x] = value[:, 0:NP]
            main_out[i, x] = value[:, NP:]
        stream_plane(1, x, slice(0, LANES), write)

    def rows_start(step):
        @pl.when(st == 0)
        def _():
            for d in range(1, ROWS):
                row_copy(step, d).start()
            rows_buf[step][0] = star[step, 0:5, CX, :, 0:NP]

    small_row = lax.broadcasted_iota(jnp.int32, (CZ, 128), 0)

    def row_slot(tile):
        return lax.rem(row - lax.div(tile, COLS) + ROWS, ROWS)

    def col_slot(tile):
        return lax.rem(col - lax.rem(tile, COLS) + COLS, COLS)

    def quads_start(step):
        @pl.when(st == 0)
        def _():
            for d in range(1, ROWS):
                row_copy(step, d).wait_recv()
            for e in range(COLS):
                target = row * COLS + lax.rem(col + e, COLS)
                own = tile_ref[target]
                left = tile_ref[lax.rem(target + SPAN - 1, SPAN)]
                right = tile_ref[lax.rem(target + 1, SPAN)]
                out = pay_recv[step].at[0] if e == 0 else pay_send.at[step, e]
                out[0:5] = rows_buf[step][row_slot(own)]
                out[5] = jnp.where(
                    small_row == 0,
                    pltpu.roll(rows_buf[step][row_slot(left), 3], 1, 0),
                    pltpu.roll(rows_buf[step][row_slot(right), 4], 1, 0))
                if e:
                    quad_copy(step, e).start()

    def inlet(step):
        @pl.when(st == 0)
        def _():
            for e in range(1, COLS):
                quad_copy(step, e).wait_recv()
            left_at = lax.rem(sp + SPAN - 1, SPAN)
            right_at = lax.rem(sp + 1, SPAN)
            tile = pay_recv[step][col_slot(tile_ref[sp]), 0:5]
            edge = jnp.where(small_row == 0,
                             pay_recv[step][col_slot(tile_ref[left_at]), 5],
                             pay_recv[step][col_slot(tile_ref[right_at]), 5])
            coarse = jnp.concatenate([tile.reshape(5 * CZ, 128), edge], axis=0)
            high = coarse.astype(jnp.bfloat16)
            rest = coarse - high.astype(jnp.float32)
            middle = rest.astype(jnp.bfloat16)
            low = (rest - middle.astype(jnp.float32)).astype(jnp.bfloat16)
            parts = jnp.dot(jnp.concatenate([high, middle, low], axis=0), spread[...],
                            preferred_element_type=jnp.float32)
            count = 6 * CZ
            fine = parts[0:count] + (parts[count:2 * count] + parts[2 * count:])
            own_phase = jnp.full((5 * CZ, NM), phase_ref[sp], jnp.int32)
            plane = jnp.where(own_phase == 0, fine[0:5 * CZ, 0:NM], fine[0:5 * CZ, NM:])
            plane = plane.reshape(5, CZ, NM)
            for k in range(5):
                star[step, k, 0, :, NP:] = plane[k]
            tail = fine[5 * CZ:, :]
            left_phase = jnp.full((CZ, NM), phase_ref[left_at], jnp.int32)
            right_phase = jnp.full((CZ, NM), phase_ref[right_at], jnp.int32)
            left = jnp.where(left_phase == 0, tail[:, 0:NM], tail[:, NM:])
            right = jnp.where(right_phase == 0, tail[:, 0:NM], tail[:, NM:])
            zrecv[step, 0, Z_UP.index(11), 0, :, NP:] = left[0:1]
            zrecv[step, 1, Z_DOWN.index(13), 0, :, NP:] = right[1:2]

    def outlet(step):
        @pl.when(st == STREAM - 1)
        def _():
            for k in range(5, 10):
                star[step, k, CX + 1, :, NP:] = star[step, k, CX, :, NP:]
            for way, pop in ((0, Z_UP.index(14)), (1, Z_DOWN.index(12))):
                zrecv[step, way, pop, CX + 1, :, NP:] = zrecv[step, way, pop, CX, :, NP:]

    for load in loads:
        load.wait()

    def first(x, carry):
        collide_planes(load_input, store_star(0), x)
        return carry

    lax.fori_loop(0, CX, first, 0)

    @pl.when(st == 0)
    def _():
        pl.semaphore_wait(barrier, 8 + ROWS + COLS - 2)

    @pl.when(st != 0)
    def _():
        pl.semaphore_wait(barrier, 8)

    def start(*copies):
        for copy in copies:
            copy.start()

    def arrive(*copies):
        for copy in copies:
            copy.wait_recv()

    rows_start(0)
    start(corner_copy(0, 1), corner_copy(0, 2), x_copy(0, 1, 0), z_copy(0, 0), z_copy(0, 1),
          x_copy(0, 0, 0), corner_copy(0, 0), corner_copy(0, 3), x_copy(0, 1, 1), x_copy(0, 0, 1))

    wall = jnp.broadcast_to(wall_ref[...].astype(jnp.float32), (CZ, NM))
    fine_id = lax.broadcasted_iota(jnp.int32, (NM, NP), 0)
    coarse_id = lax.broadcasted_iota(jnp.int32, (NM, NP), 1)
    pick = jnp.where(lax.shift_right_logical(fine_id, 1) == coarse_id, 1.0, 0.0)
    merged = jnp.dot(wall, pick, preferred_element_type=jnp.float32)
    coarse_wall = jnp.where(merged > 0.5, 1.0, 0.0)
    solid = jnp.concatenate([coarse_wall, wall], axis=1)
    lane_id = lax.broadcasted_iota(jnp.int32, (CZ, LANES), 1)
    masks[0] = solid
    masks[1] = jnp.where((lane_id == 0) | (lane_id == NP), 1.0, pltpu.roll(solid, 1, 1))
    masks[2] = jnp.where((lane_id == NP - 1) | (lane_id == LANES - 1), 1.0,
                         pltpu.roll(solid, LANES - 1, 1))

    @pl.when(st == 0)
    def _():
        coarse_row = lax.broadcasted_iota(jnp.int32, (NP, NM), 0)
        fine_col = lax.broadcasted_iota(jnp.int32, (NP, NM), 1)
        for phase in range(2):
            place = fine_col + phase
            lower = lax.shift_right_arithmetic(place - 1, 1)
            upper = jnp.where((place & 1) == 0, 0.75, 0.25)
            low = jnp.clip(lower, 0, NP - 1)
            high = jnp.clip(lower + 1, 0, NP - 1)
            spread[:, phase * NM:(phase + 1) * NM] = (
                jnp.where(coarse_row == low, 1.0 - upper, 0.0)
                + jnp.where(coarse_row == high, upper, 0.0)).astype(jnp.bfloat16)

    def inside(plane):
        def inner(x, carry):
            plane(x)
            return carry
        lax.fori_loop(1, CX - 1, inner, 0)

    arrive(z_copy(0, 0), z_copy(0, 1), corner_copy(0, 1), corner_copy(0, 2), x_copy(0, 1, 0))
    advance(CX - 1, PRE)
    rows_start(1)
    start(x_copy(1, 0, 0))
    inside(advance)
    arrive(x_copy(0, 1, 1))
    outlet(0)
    advance(CX - 1, MAIN)
    start(x_copy(1, 0, 1), corner_copy(1, 0), corner_copy(1, 3))
    quads_start(0)
    arrive(x_copy(0, 0, 0), x_copy(0, 0, 1), corner_copy(0, 0), corner_copy(0, 3))
    inlet(0)
    advance(0)
    start(z_copy(1, 0), z_copy(1, 1), corner_copy(1, 1), corner_copy(1, 2),
          x_copy(1, 1, 0), x_copy(1, 1, 1))

    quads_start(1)
    arrive(z_copy(1, 0), z_copy(1, 1))
    inside(finish)
    arrive(corner_copy(1, 1), corner_copy(1, 2), x_copy(1, 1, 0), x_copy(1, 1, 1))
    outlet(1)
    finish(CX - 1)
    arrive(x_copy(1, 0, 0), x_copy(1, 0, 1), corner_copy(1, 0), corner_copy(1, 3))
    inlet(1)
    finish(0)

    for step in range(2):
        for way in range(2):
            z_copy(step, way).wait_send()
            for part in range(2):
                x_copy(step, way, part).wait_send()
        for which in range(4):
            corner_copy(step, which).wait_send()

    @pl.when(st == 0)
    def _():
        for step in range(2):
            for d in range(1, ROWS):
                row_copy(step, d).wait_send()
            for e in range(1, COLS):
                quad_copy(step, e).wait_send()


def local(pre_pops, main_pops, tile_map, layer_phase, wall_flags):
    vmem = pl.BlockSpec(memory_space=pltpu.VMEM)
    hbm = pl.BlockSpec(memory_space=pltpu.HBM)
    dma = pltpu.SemaphoreType.DMA
    f32 = jnp.float32
    return pl.pallas_call(
        body,
        out_shape=(jax.ShapeDtypeStruct(pre_pops.shape, f32),
                   jax.ShapeDtypeStruct(main_pops.shape, f32)),
        in_specs=[hbm] * 5,
        out_specs=(vmem, vmem),
        scratch_shapes=[
            pltpu.SMEM((SPAN,), jnp.int32),
            pltpu.SMEM((SPAN,), jnp.int32),
            pltpu.VMEM((1, NM), jnp.int32),
            pltpu.VMEM((19, CX, CZ, NP), f32),
            pltpu.VMEM((19, CX, CZ, NM), f32),
            pltpu.VMEM((2, 19, CX + 2, CZ, LANES), f32),
            pltpu.VMEM((2, 2, 5, CX, 1, LANES), f32),
            pltpu.VMEM((2, 2, 5, CX + 2, 1, LANES), f32),
            pltpu.VMEM((19, CZ, LANES), f32),
            pltpu.VMEM((3, CZ, LANES), f32),
            pltpu.VMEM((NP, 2 * NM), jnp.bfloat16),
            pltpu.VMEM((ROWS, 5, CZ, NP), f32),
            pltpu.VMEM((ROWS, 5, CZ, NP), f32),
            pltpu.VMEM((2, COLS, 6, CZ, NP), f32),
            pltpu.VMEM((COLS, 6, CZ, NP), f32),
            pltpu.VMEM((COLS, 6, CZ, NP), f32),
            dma((2, 2, 2)), dma((2, 2, 2)), dma((2, 2)), dma((2, 2)),
            dma((2, 4)), dma((2, 4)),
            dma((2, ROWS)), dma((2, ROWS)), dma((2, COLS)), dma((2, COLS)), dma((5,)),
        ],
        compiler_params=pltpu.CompilerParams(
            collective_id=0, has_side_effects=True, vmem_limit_bytes=20 * 1024 * 1024),
    )(*[pltpu.with_memory_space_constraint(array, pltpu.HBM) for array in (
        tile_map, layer_phase, wall_flags.reshape(1, NM), pre_pops, main_pops)])


def solution(mesh):
    spec = jax.sharding.PartitionSpec
    blocks = spec(None, "stream", "span", None)
    return jax.shard_map(
        local,
        mesh=mesh,
        in_specs=(blocks, blocks, spec(), spec(), spec()),
        out_specs=(blocks, blocks),
        check_vma=False,
    )
```

```python
import jax
import jax.numpy as jnp
from jax import lax
from jax.experimental import pallas as pl
from jax.experimental.pallas import tpu as pltpu

VELOCITIES = (
    (0, 0, 0),
    (1, 0, 0), (-1, 0, 0), (0, 1, 0), (0, -1, 0), (0, 0, 1), (0, 0, -1),
    (1, 1, 0), (-1, -1, 0), (1, -1, 0), (-1, 1, 0),
    (1, 0, 1), (-1, 0, -1), (1, 0, -1), (-1, 0, 1),
    (0, 1, 1), (0, -1, -1), (0, 1, -1), (0, -1, 1),
)
OPPOSITE = (0, 2, 1, 4, 3, 6, 5, 8, 7, 10, 9, 12, 11, 14, 13, 16, 15, 18, 17)
ORDER = (1, 7, 9, 11, 13, 2, 8, 10, 12, 14, 0, 3, 4, 5, 6, 15, 16, 17, 18)
POS = tuple(ORDER.index(i) for i in range(19))
Z_UP = (5, 11, 14, 15, 18)
Z_DOWN = (6, 12, 13, 16, 17)
PAIRS = ((1, 2), (3, 4), (5, 6), (7, 8), (9, 10), (11, 12), (13, 14), (15, 16), (17, 18))
CX, CZ = 8, 8
NP, NM = 128, 256
LANES = NP + NM
STREAM, SPAN = 16, 32
ROWS, COLS = 8, 4
MESH = pl.DeviceIdType.MESH


def collide_planes(load, store, x, chunks=(0, 1, 2)):
    for lane in chunks:
        g = [load(i, x, lane) for i in range(19)]
        diff = {a: g[a] - g[b] for a, b in PAIRS}
        both = {a: g[a] + g[b] for a, b in PAIRS}
        axes = both[1] + both[3] + both[5]
        edges = (both[7] + both[9]) + (both[11] + both[13]) + (both[15] + both[17])
        density = (1.0 / 3.0) * g[0] + (1.0 / 18.0) * axes + (1.0 / 36.0) * edges
        mx = (1.0 / 18.0) * diff[1] + (1.0 / 36.0) * ((diff[7] + diff[9]) + (diff[11] + diff[13]))
        my = (1.0 / 18.0) * diff[3] + (1.0 / 36.0) * ((diff[7] - diff[9]) + (diff[15] + diff[17]))
        mz = (1.0 / 18.0) * diff[5] + (1.0 / 36.0) * ((diff[11] - diff[13]) + (diff[15] - diff[17]))
        inverse = 1.0 / density
        base = 1.25 * density - (1.875 * inverse) * (mx * mx + my * my + mz * mz)
        scale = 5.625 * inverse
        store(0, x, lane, base - 0.25 * g[0])
        moment = (mx, my, mz)
        for a, b in PAIRS:
            along = None
            for axis in range(3):
                c = VELOCITIES[a][axis]
                if c:
                    term = moment[axis]
                    if along is None:
                        along = term
                    else:
                        along = along + term if c > 0 else along - term
            even = base + scale * (along * along)
            odd = 3.75 * along
            store(a, x, lane, (even + odd) - 0.25 * g[a])
            store(b, x, lane, (even - odd) - 0.25 * g[b])


def body(tile_hbm, phase_hbm, wall_hbm, pre_hbm, main_hbm, pre_out, main_out,
         tile_ref, phase_ref, wall_ref, pre_ref, main_ref, star, zsend, zrecv, temp, masks, spread, rows_a, rows_b, pay_send, pay_a, pay_b,
         xs_sem, xr_sem, zs_sem, zr_sem, cs_sem, cr_sem, ys_sem, yr_sem, qs_sem, qr_sem, in_sem, ready_sem):
    rows_buf, pay_recv = (rows_a, rows_b), (pay_a, pay_b)
    st = lax.axis_index("stream")
    sp = lax.axis_index("span")
    st_up, st_down = lax.rem(st + 1, STREAM), lax.rem(st + STREAM - 1, STREAM)
    sp_up, sp_down = lax.rem(sp + 1, SPAN), lax.rem(sp + SPAN - 1, SPAN)
    row, col = lax.div(sp, COLS), lax.rem(sp, COLS)

    barrier = pltpu.get_barrier_semaphore()
    for a, b in ((st, sp_up), (st, sp_down), (st_down, sp_up), (st_down, sp), (st_down, sp_down)):
        pl.semaphore_signal(barrier, inc=1, device_id=(a, b), device_id_type=MESH)

    @pl.when(st != STREAM - 1)
    def _():
        for b in (sp_up, sp, sp_down):
            pl.semaphore_signal(barrier, inc=1, device_id=(st_up, b), device_id_type=MESH)

    @pl.when(st == 0)
    def _():
        for d in range(1, ROWS):
            peer = lax.rem(row + d, ROWS) * COLS + col
            pl.semaphore_signal(barrier, inc=1, device_id=(st, peer), device_id_type=MESH)
        for e in range(1, COLS):
            peer = row * COLS + lax.rem(col + e, COLS)
            pl.semaphore_signal(barrier, inc=1, device_id=(st, peer), device_id_type=MESH)

    loads = [pltpu.make_async_copy(source, target, in_sem.at[at])
             for at, (source, target) in enumerate((
                 (pre_hbm, pre_ref), (main_hbm, main_ref), (wall_hbm, wall_ref),
                 (tile_hbm, tile_ref), (phase_hbm, phase_ref)))]
    for load in loads:
        load.start()

    def remote(src, dst, send, recv, device):
        return pltpu.make_async_remote_copy(
            src_ref=src, dst_ref=dst, send_sem=send, recv_sem=recv,
            device_id=device, device_id_type=MESH)

    PRE, MAIN = slice(0, NP), slice(NP, LANES)

    def x_copy(step, way, part):
        cut = (PRE, MAIN)[part]
        if way == 0:
            return remote(star.at[step, 0:5, CX, :, cut], star.at[step, 0:5, 0, :, cut],
                          xs_sem.at[step, 0, part], xr_sem.at[step, 0, part], (st_up, sp))
        return remote(star.at[step, 5:10, 1, :, cut], star.at[step, 5:10, CX + 1, :, cut],
                      xs_sem.at[step, 1, part], xr_sem.at[step, 1, part], (st_down, sp))

    def z_copy(step, way):
        return remote(zsend.at[step, way], zrecv.at[step, way, :, 1:CX + 1],
                      zs_sem.at[step, way], zr_sem.at[step, way],
                      (st, sp_up if way == 0 else sp_down))

    def corner_copy(step, which):
        way, pop, x, slot, device = (
            (0, Z_UP.index(11), CX - 1, 0, (st_up, sp_up)),
            (0, Z_UP.index(14), 0, CX + 1, (st_down, sp_up)),
            (1, Z_DOWN.index(12), 0, CX + 1, (st_down, sp_down)),
            (1, Z_DOWN.index(13), CX - 1, 0, (st_up, sp_down)),
        )[which]
        return remote(zsend.at[step, way, pop, x], zrecv.at[step, way, pop, slot],
                      cs_sem.at[step, which], cr_sem.at[step, which], device)

    def row_copy(step, d):
        peer = lax.rem(row + d, ROWS) * COLS + col
        return remote(star.at[step, 0:5, CX, :, 0:NP], rows_buf[step].at[d],
                      ys_sem.at[step, d], yr_sem.at[step, d], (st, peer))

    def quad_copy(step, e):
        peer = row * COLS + lax.rem(col + e, COLS)
        return remote(pay_send.at[step, e], pay_recv[step].at[e],
                      qs_sem.at[step, e], qr_sem.at[step, e], (st, peer))

    def lanes(lane):
        return slice(lane * 128, lane * 128 + 128)

    def load_input(i, x, lane):
        if lane == 0:
            return pre_ref[i, x]
        return main_ref[i, x, :, lanes(lane - 1)]

    def load_temp(i, x, lane):
        return temp[i, :, lanes(lane)]

    def store_star(step):
        def store(i, x, lane, value):
            star[step, POS[i], x + 1, :, lanes(lane)] = value
            if i in Z_UP:
                zsend[step, 0, Z_UP.index(i), x, :, lanes(lane)] = value[CZ - 1:CZ, :]
            if i in Z_DOWN:
                zsend[step, 1, Z_DOWN.index(i), x, :, lanes(lane)] = value[0:1, :]
        return store

    def stream_plane(step, x, cut, write):
        width = cut.stop - cut.start
        row_id = lax.broadcasted_iota(jnp.int32, (CZ, width), 0)
        for i in range(19):
            cx, cy, cz = VELOCITIES[i]
            source = star[step, POS[i], x + 1 - cx, :, cut]
            if cz == 1:
                edge = zrecv[step, 0, Z_UP.index(i), x + 1 - cx, :, cut]
                source = jnp.where(row_id == 0, jnp.broadcast_to(edge, (CZ, width)),
                                   pltpu.roll(source, 1, 0))
            elif cz == -1:
                edge = zrecv[step, 1, Z_DOWN.index(i), x + 1 - cx, :, cut]
                source = jnp.where(row_id == CZ - 1, jnp.broadcast_to(edge, (CZ, width)),
                                   pltpu.roll(source, CZ - 1, 0))
            if cy == 1:
                source = pltpu.roll(source, 1, 1)
            elif cy == -1:
                source = pltpu.roll(source, width - 1, 1)
            bounced = star[step, POS[OPPOSITE[i]], x + 1, :, cut]
            write(i, jnp.where(masks[cy % 3, :, cut] > 0.5, bounced, source))

    def advance(x, cut=slice(0, LANES)):
        def write(i, value):
            temp[i, :, cut] = value
        stream_plane(0, x, cut, write)
        collide_planes(load_temp, store_star(1), x, range(cut.start // 128, cut.stop // 128))

    def finish(x):
        def write(i, value):
            pre_out[i, x] = value[:, 0:NP]
            main_out[i, x] = value[:, NP:]
        stream_plane(1, x, slice(0, LANES), write)

    def rows_start(step):
        @pl.when(st == 0)
        def _():
            for d in (4, 3, 5, 2, 6, 1, 7):
                row_copy(step, d).start()
            rows_buf[step][0] = star[step, 0:5, CX, :, 0:NP]

    small_row = lax.broadcasted_iota(jnp.int32, (CZ, 128), 0)

    def row_slot(tile):
        return lax.rem(row - lax.div(tile, COLS) + ROWS, ROWS)

    def col_slot(tile):
        return lax.rem(col - lax.rem(tile, COLS) + COLS, COLS)

    def quads_start(step):
        @pl.when(st == 0)
        def _():
            for d in range(1, ROWS):
                row_copy(step, d).wait_recv()
            for e in range(COLS):
                target = row * COLS + lax.rem(col + e, COLS)
                own = tile_ref[target]
                left = tile_ref[lax.rem(target + SPAN - 1, SPAN)]
                right = tile_ref[lax.rem(target + 1, SPAN)]
                out = pay_recv[step].at[0] if e == 0 else pay_send.at[step, e]
                out[0:5] = rows_buf[step][row_slot(own)]
                out[5] = jnp.where(
                    small_row == 0,
                    pltpu.roll(rows_buf[step][row_slot(left), 3], 1, 0),
                    pltpu.roll(rows_buf[step][row_slot(right), 4], 1, 0))
                if e:
                    quad_copy(step, e).start()

    def inlet(step):
        @pl.when(st == 0)
        def _():
            for e in range(1, COLS):
                quad_copy(step, e).wait_recv()
            left_at = lax.rem(sp + SPAN - 1, SPAN)
            right_at = lax.rem(sp + 1, SPAN)
            tile = pay_recv[step][col_slot(tile_ref[sp]), 0:5]
            edge = jnp.where(small_row == 0,
                             pay_recv[step][col_slot(tile_ref[left_at]), 5],
                             pay_recv[step][col_slot(tile_ref[right_at]), 5])
            coarse = jnp.concatenate([tile.reshape(5 * CZ, 128), edge], axis=0)
            high = coarse.astype(jnp.bfloat16)
            rest = coarse - high.astype(jnp.float32)
            middle = rest.astype(jnp.bfloat16)
            low = (rest - middle.astype(jnp.float32)).astype(jnp.bfloat16)
            parts = jnp.dot(jnp.concatenate([high, middle, low], axis=0), spread[...],
                            preferred_element_type=jnp.float32)
            count = 6 * CZ
            fine = parts[0:count] + (parts[count:2 * count] + parts[2 * count:])
            own_phase = jnp.full((5 * CZ, NM), phase_ref[sp], jnp.int32)
            plane = jnp.where(own_phase == 0, fine[0:5 * CZ, 0:NM], fine[0:5 * CZ, NM:])
            plane = plane.reshape(5, CZ, NM)
            for k in range(5):
                star[step, k, 0, :, NP:] = plane[k]
            tail = fine[5 * CZ:, :]
            left_phase = jnp.full((CZ, NM), phase_ref[left_at], jnp.int32)
            right_phase = jnp.full((CZ, NM), phase_ref[right_at], jnp.int32)
            left = jnp.where(left_phase == 0, tail[:, 0:NM], tail[:, NM:])
            right = jnp.where(right_phase == 0, tail[:, 0:NM], tail[:, NM:])
            zrecv[step, 0, Z_UP.index(11), 0, :, NP:] = left[0:1]
            zrecv[step, 1, Z_DOWN.index(13), 0, :, NP:] = right[1:2]

    def outlet(step):
        @pl.when(st == STREAM - 1)
        def _():
            for k in range(5, 10):
                star[step, k, CX + 1, :, NP:] = star[step, k, CX, :, NP:]
            for way, pop in ((0, Z_UP.index(14)), (1, Z_DOWN.index(12))):
                zrecv[step, way, pop, CX + 1, :, NP:] = zrecv[step, way, pop, CX, :, NP:]

    for load in loads:
        load.wait()

    def first(x, carry):
        collide_planes(load_input, store_star(0), x)
        return carry

    lax.fori_loop(0, CX, first, 0)

    @pl.when(st == 0)
    def _():
        pl.semaphore_wait(barrier, 5 + ROWS + COLS - 2)

    @pl.when(st != 0)
    def _():
        pl.semaphore_wait(barrier, 8)

    @pl.when(st == STREAM - 1)
    def _():
        for b in (sp_up, sp, sp_down):
            pl.semaphore_signal(ready_sem, inc=1, device_id=(st_up, b), device_id_type=MESH)

    def start(*copies):
        for copy in copies:
            copy.start()

    def arrive(*copies):
        for copy in copies:
            copy.wait_recv()

    rows_start(0)

    @pl.when(st != 0)
    def _():
        start(corner_copy(0, 1), corner_copy(0, 2), x_copy(0, 1, 0))

    start(z_copy(0, 0), z_copy(0, 1), x_copy(0, 0, 0), corner_copy(0, 0), corner_copy(0, 3))

    @pl.when(st != 0)
    def _():
        start(x_copy(0, 1, 1))

    start(x_copy(0, 0, 1))

    wall = jnp.broadcast_to(wall_ref[...].astype(jnp.float32), (CZ, NM))
    fine_id = lax.broadcasted_iota(jnp.int32, (NM, NP), 0)
    coarse_id = lax.broadcasted_iota(jnp.int32, (NM, NP), 1)
    pick = jnp.where(lax.shift_right_logical(fine_id, 1) == coarse_id, 1.0, 0.0)
    merged = jnp.dot(wall, pick, preferred_element_type=jnp.float32)
    coarse_wall = jnp.where(merged > 0.5, 1.0, 0.0)
    solid = jnp.concatenate([coarse_wall, wall], axis=1)
    lane_id = lax.broadcasted_iota(jnp.int32, (CZ, LANES), 1)
    masks[0] = solid
    masks[1] = jnp.where((lane_id == 0) | (lane_id == NP), 1.0, pltpu.roll(solid, 1, 1))
    masks[2] = jnp.where((lane_id == NP - 1) | (lane_id == LANES - 1), 1.0,
                         pltpu.roll(solid, LANES - 1, 1))

    @pl.when(st == 0)
    def _():
        coarse_row = lax.broadcasted_iota(jnp.int32, (NP, NM), 0)
        fine_col = lax.broadcasted_iota(jnp.int32, (NP, NM), 1)
        for phase in range(2):
            place = fine_col + phase
            lower = lax.shift_right_arithmetic(place - 1, 1)
            upper = jnp.where((place & 1) == 0, 0.75, 0.25)
            low = jnp.clip(lower, 0, NP - 1)
            high = jnp.clip(lower + 1, 0, NP - 1)
            spread[:, phase * NM:(phase + 1) * NM] = (
                jnp.where(coarse_row == low, 1.0 - upper, 0.0)
                + jnp.where(coarse_row == high, upper, 0.0)).astype(jnp.bfloat16)

    def inside(plane):
        def inner(x, carry):
            plane(x)
            return carry
        lax.fori_loop(1, CX - 1, inner, 0)

    arrive(z_copy(0, 0), z_copy(0, 1), corner_copy(0, 1), corner_copy(0, 2), x_copy(0, 1, 0))
    advance(CX - 1, PRE)
    rows_start(1)
    start(x_copy(1, 0, 0))
    inside(advance)
    arrive(x_copy(0, 1, 1))
    outlet(0)
    advance(CX - 1, MAIN)
    start(x_copy(1, 0, 1), corner_copy(1, 0), corner_copy(1, 3))
    quads_start(0)

    @pl.when(st == 0)
    def _():
        pl.semaphore_wait(ready_sem, 3)
        start(corner_copy(0, 1), corner_copy(0, 2), x_copy(0, 1, 0), x_copy(0, 1, 1))

    arrive(x_copy(0, 0, 0), x_copy(0, 0, 1), corner_copy(0, 0), corner_copy(0, 3))
    inlet(0)
    advance(0)
    start(z_copy(1, 0), z_copy(1, 1), corner_copy(1, 1), corner_copy(1, 2),
          x_copy(1, 1, 0), x_copy(1, 1, 1))

    quads_start(1)
    arrive(z_copy(1, 0), z_copy(1, 1))
    inside(finish)
    arrive(corner_copy(1, 1), corner_copy(1, 2), x_copy(1, 1, 0), x_copy(1, 1, 1))
    outlet(1)
    finish(CX - 1)
    arrive(x_copy(1, 0, 0), x_copy(1, 0, 1), corner_copy(1, 0), corner_copy(1, 3))
    inlet(1)
    finish(0)

    for step in range(2):
        for way in range(2):
            z_copy(step, way).wait_send()
            for part in range(2):
                x_copy(step, way, part).wait_send()
        for which in range(4):
            corner_copy(step, which).wait_send()

    @pl.when(st == 0)
    def _():
        for step in range(2):
            for d in range(1, ROWS):
                row_copy(step, d).wait_send()
            for e in range(1, COLS):
                quad_copy(step, e).wait_send()


def local(pre_pops, main_pops, tile_map, layer_phase, wall_flags):
    vmem = pl.BlockSpec(memory_space=pltpu.VMEM)
    hbm = pl.BlockSpec(memory_space=pltpu.HBM)
    dma = pltpu.SemaphoreType.DMA
    f32 = jnp.float32
    return pl.pallas_call(
        body,
        out_shape=(jax.ShapeDtypeStruct(pre_pops.shape, f32),
                   jax.ShapeDtypeStruct(main_pops.shape, f32)),
        in_specs=[hbm] * 5,
        out_specs=(vmem, vmem),
        scratch_shapes=[
            pltpu.SMEM((SPAN,), jnp.int32),
            pltpu.SMEM((SPAN,), jnp.int32),
            pltpu.VMEM((1, NM), jnp.int32),
            pltpu.VMEM((19, CX, CZ, NP), f32),
            pltpu.VMEM((19, CX, CZ, NM), f32),
            pltpu.VMEM((2, 19, CX + 2, CZ, LANES), f32),
            pltpu.VMEM((2, 2, 5, CX, 1, LANES), f32),
            pltpu.VMEM((2, 2, 5, CX + 2, 1, LANES), f32),
            pltpu.VMEM((19, CZ, LANES), f32),
            pltpu.VMEM((3, CZ, LANES), f32),
            pltpu.VMEM((NP, 2 * NM), jnp.bfloat16),
            pltpu.VMEM((ROWS, 5, CZ, NP), f32),
            pltpu.VMEM((ROWS, 5, CZ, NP), f32),
            pltpu.VMEM((2, COLS, 6, CZ, NP), f32),
            pltpu.VMEM((COLS, 6, CZ, NP), f32),
            pltpu.VMEM((COLS, 6, CZ, NP), f32),
            dma((2, 2, 2)), dma((2, 2, 2)), dma((2, 2)), dma((2, 2)),
            dma((2, 4)), dma((2, 4)),
            dma((2, ROWS)), dma((2, ROWS)), dma((2, COLS)), dma((2, COLS)), dma((5,)), pltpu.SemaphoreType.REGULAR,
        ],
        compiler_params=pltpu.CompilerParams(
            collective_id=0, has_side_effects=True, vmem_limit_bytes=20 * 1024 * 1024),
    )(*[pltpu.with_memory_space_constraint(array, pltpu.HBM) for array in (
        tile_map, layer_phase, wall_flags.reshape(1, NM), pre_pops, main_pops)])


def solution(mesh):
    spec = jax.sharding.PartitionSpec
    blocks = spec(None, "stream", "span", None)
    return jax.shard_map(
        local,
        mesh=mesh,
        in_specs=(blocks, blocks, spec(), spec(), spec()),
        out_specs=(blocks, blocks),
        check_vma=False,
    )
```

```python
import jax
import jax.numpy as jnp
from jax import lax
from jax.experimental import pallas as pl
from jax.experimental.pallas import tpu as pltpu

VELOCITIES = (
    (0, 0, 0),
    (1, 0, 0), (-1, 0, 0), (0, 1, 0), (0, -1, 0), (0, 0, 1), (0, 0, -1),
    (1, 1, 0), (-1, -1, 0), (1, -1, 0), (-1, 1, 0),
    (1, 0, 1), (-1, 0, -1), (1, 0, -1), (-1, 0, 1),
    (0, 1, 1), (0, -1, -1), (0, 1, -1), (0, -1, 1),
)
OPPOSITE = (0, 2, 1, 4, 3, 6, 5, 8, 7, 10, 9, 12, 11, 14, 13, 16, 15, 18, 17)
ORDER = (1, 7, 9, 11, 13, 2, 8, 10, 12, 14, 0, 3, 4, 5, 6, 15, 16, 17, 18)
POS = tuple(ORDER.index(i) for i in range(19))
Z_UP = (5, 11, 14, 15, 18)
Z_DOWN = (6, 12, 13, 16, 17)
PAIRS = ((1, 2), (3, 4), (5, 6), (7, 8), (9, 10), (11, 12), (13, 14), (15, 16), (17, 18))
CX, CZ = 8, 8
NP, NM = 128, 256
LANES = NP + NM
STREAM, SPAN = 16, 32
ROWS, COLS = 8, 4
MESH = pl.DeviceIdType.MESH


def collide_planes(load, store, x, chunks=(0, 1, 2)):
    for lane in chunks:
        g = [load(i, x, lane) for i in range(19)]
        diff = {a: g[a] - g[b] for a, b in PAIRS}
        both = {a: g[a] + g[b] for a, b in PAIRS}
        axes = both[1] + both[3] + both[5]
        edges = (both[7] + both[9]) + (both[11] + both[13]) + (both[15] + both[17])
        density = (1.0 / 3.0) * g[0] + (1.0 / 18.0) * axes + (1.0 / 36.0) * edges
        mx = (1.0 / 18.0) * diff[1] + (1.0 / 36.0) * ((diff[7] + diff[9]) + (diff[11] + diff[13]))
        my = (1.0 / 18.0) * diff[3] + (1.0 / 36.0) * ((diff[7] - diff[9]) + (diff[15] + diff[17]))
        mz = (1.0 / 18.0) * diff[5] + (1.0 / 36.0) * ((diff[11] - diff[13]) + (diff[15] - diff[17]))
        inverse = 1.0 / density
        base = 1.25 * density - (1.875 * inverse) * (mx * mx + my * my + mz * mz)
        scale = 5.625 * inverse
        store(0, x, lane, base - 0.25 * g[0])
        moment = (mx, my, mz)
        for a, b in PAIRS:
            along = None
            for axis in range(3):
                c = VELOCITIES[a][axis]
                if c:
                    term = moment[axis]
                    if along is None:
                        along = term
                    else:
                        along = along + term if c > 0 else along - term
            even = base + scale * (along * along)
            odd = 3.75 * along
            store(a, x, lane, (even + odd) - 0.25 * g[a])
            store(b, x, lane, (even - odd) - 0.25 * g[b])


def body(tile_hbm, phase_hbm, wall_hbm, pre_hbm, main_hbm, pre_out, main_out,
         tile_ref, phase_ref, wall_ref, pre_ref, main_ref, star, zsend, zrecv, temp, masks, spread, rows_a, rows_b, pay_send, pay_a, pay_b,
         xs_sem, xr_sem, zs_sem, zr_sem, cs_sem, cr_sem, ys_sem, yr_sem, qs_sem, qr_sem, in_sem, ready_sem):
    rows_buf, pay_recv = (rows_a, rows_b), (pay_a, pay_b)
    st = lax.axis_index("stream")
    sp = lax.axis_index("span")
    st_up, st_down = lax.rem(st + 1, STREAM), lax.rem(st + STREAM - 1, STREAM)
    sp_up, sp_down = lax.rem(sp + 1, SPAN), lax.rem(sp + SPAN - 1, SPAN)
    row, col = lax.div(sp, COLS), lax.rem(sp, COLS)

    barrier = pltpu.get_barrier_semaphore()
    for a, b in ((st, sp_up), (st, sp_down), (st_down, sp_up), (st_down, sp), (st_down, sp_down)):
        pl.semaphore_signal(barrier, inc=1, device_id=(a, b), device_id_type=MESH)

    @pl.when(st != STREAM - 1)
    def _():
        for b in (sp_up, sp, sp_down):
            pl.semaphore_signal(barrier, inc=1, device_id=(st_up, b), device_id_type=MESH)

    @pl.when(st == 0)
    def _():
        for d in range(1, ROWS):
            peer = lax.rem(row + d, ROWS) * COLS + col
            pl.semaphore_signal(barrier, inc=1, device_id=(st, peer), device_id_type=MESH)
        for e in range(1, COLS):
            peer = row * COLS + lax.rem(col + e, COLS)
            pl.semaphore_signal(barrier, inc=1, device_id=(st, peer), device_id_type=MESH)

    loads = [pltpu.make_async_copy(source, target, in_sem.at[at])
             for at, (source, target) in enumerate((
                 (pre_hbm, pre_ref), (main_hbm, main_ref), (wall_hbm, wall_ref),
                 (tile_hbm, tile_ref), (phase_hbm, phase_ref)))]
    for load in loads:
        load.start()

    def remote(src, dst, send, recv, device):
        return pltpu.make_async_remote_copy(
            src_ref=src, dst_ref=dst, send_sem=send, recv_sem=recv,
            device_id=device, device_id_type=MESH)

    PRE, MAIN = slice(0, NP), slice(NP, LANES)

    def x_copy(step, way, part):
        cut = (PRE, MAIN)[part]
        if way == 0:
            return remote(star.at[step, 0:5, CX, :, cut], star.at[step, 0:5, 0, :, cut],
                          xs_sem.at[step, 0, part], xr_sem.at[step, 0, part], (st_up, sp))
        return remote(star.at[step, 5:10, 1, :, cut], star.at[step, 5:10, CX + 1, :, cut],
                      xs_sem.at[step, 1, part], xr_sem.at[step, 1, part], (st_down, sp))

    def z_copy(step, way):
        return remote(zsend.at[step, way], zrecv.at[step, way, :, 1:CX + 1],
                      zs_sem.at[step, way], zr_sem.at[step, way],
                      (st, sp_up if way == 0 else sp_down))

    def corner_copy(step, which):
        way, pop, x, slot, device = (
            (0, Z_UP.index(11), CX - 1, 0, (st_up, sp_up)),
            (0, Z_UP.index(14), 0, CX + 1, (st_down, sp_up)),
            (1, Z_DOWN.index(12), 0, CX + 1, (st_down, sp_down)),
            (1, Z_DOWN.index(13), CX - 1, 0, (st_up, sp_down)),
        )[which]
        return remote(zsend.at[step, way, pop, x], zrecv.at[step, way, pop, slot],
                      cs_sem.at[step, which], cr_sem.at[step, which], device)

    def row_copy(step, d):
        peer = lax.rem(row + d, ROWS) * COLS + col
        return remote(star.at[step, 0:5, CX, :, 0:NP], rows_buf[step].at[d],
                      ys_sem.at[step, d], yr_sem.at[step, d], (st, peer))

    def quad_copy(step, e):
        peer = row * COLS + lax.rem(col + e, COLS)
        return remote(pay_send.at[step, e], pay_recv[step].at[e],
                      qs_sem.at[step, e], qr_sem.at[step, e], (st, peer))

    def lanes(lane):
        return slice(lane * 128, lane * 128 + 128)

    def load_input(i, x, lane):
        if lane == 0:
            return pre_ref[i, x]
        return main_ref[i, x, :, lanes(lane - 1)]

    def load_temp(i, x, lane):
        return temp[i, :, lanes(lane)]

    def store_star(step):
        def store(i, x, lane, value):
            star[step, POS[i], x + 1, :, lanes(lane)] = value
            if i in Z_UP:
                zsend[step, 0, Z_UP.index(i), x, :, lanes(lane)] = value[CZ - 1:CZ, :]
            if i in Z_DOWN:
                zsend[step, 1, Z_DOWN.index(i), x, :, lanes(lane)] = value[0:1, :]
        return store

    def stream_plane(step, x, cut, write):
        width = cut.stop - cut.start
        row_id = lax.broadcasted_iota(jnp.int32, (CZ, width), 0)
        for i in range(19):
            cx, cy, cz = VELOCITIES[i]
            source = star[step, POS[i], x + 1 - cx, :, cut]
            if cz == 1:
                edge = zrecv[step, 0, Z_UP.index(i), x + 1 - cx, :, cut]
                source = jnp.where(row_id == 0, jnp.broadcast_to(edge, (CZ, width)),
                                   pltpu.roll(source, 1, 0))
            elif cz == -1:
                edge = zrecv[step, 1, Z_DOWN.index(i), x + 1 - cx, :, cut]
                source = jnp.where(row_id == CZ - 1, jnp.broadcast_to(edge, (CZ, width)),
                                   pltpu.roll(source, CZ - 1, 0))
            if cy == 1:
                source = pltpu.roll(source, 1, 1)
            elif cy == -1:
                source = pltpu.roll(source, width - 1, 1)
            bounced = star[step, POS[OPPOSITE[i]], x + 1, :, cut]
            write(i, jnp.where(masks[cy % 3, :, cut] > 0.5, bounced, source))

    def advance(x, cut=slice(0, LANES)):
        def write(i, value):
            temp[i, :, cut] = value
        stream_plane(0, x, cut, write)
        collide_planes(load_temp, store_star(1), x, range(cut.start // 128, cut.stop // 128))

    def finish(x):
        def write(i, value):
            pre_out[i, x] = value[:, 0:NP]
            main_out[i, x] = value[:, NP:]
        stream_plane(1, x, slice(0, LANES), write)

    def rows_start(step):
        @pl.when(st == 0)
        def _():
            for d in (4, 3, 5, 2, 6, 1, 7):
                row_copy(step, d).start()
            rows_buf[step][0] = star[step, 0:5, CX, :, 0:NP]

    small_row = lax.broadcasted_iota(jnp.int32, (CZ, 128), 0)

    def row_slot(tile):
        return lax.rem(row - lax.div(tile, COLS) + ROWS, ROWS)

    def col_slot(tile):
        return lax.rem(col - lax.rem(tile, COLS) + COLS, COLS)

    def quads_start(step):
        @pl.when(st == 0)
        def _():
            for d in range(1, ROWS):
                row_copy(step, d).wait_recv()
            for e in range(COLS):
                target = row * COLS + lax.rem(col + e, COLS)
                own = tile_ref[target]
                left = tile_ref[lax.rem(target + SPAN - 1, SPAN)]
                right = tile_ref[lax.rem(target + 1, SPAN)]
                out = pay_recv[step].at[0] if e == 0 else pay_send.at[step, e]
                out[0:5] = rows_buf[step][row_slot(own)]
                out[5] = jnp.where(
                    small_row == 0,
                    pltpu.roll(rows_buf[step][row_slot(left), 3], 1, 0),
                    pltpu.roll(rows_buf[step][row_slot(right), 4], 1, 0))
                if e:
                    quad_copy(step, e).start()

    def inlet(step):
        @pl.when(st == 0)
        def _():
            for e in range(1, COLS):
                quad_copy(step, e).wait_recv()
            left_at = lax.rem(sp + SPAN - 1, SPAN)
            right_at = lax.rem(sp + 1, SPAN)
            tile = pay_recv[step][col_slot(tile_ref[sp]), 0:5]
            edge = jnp.where(small_row == 0,
                             pay_recv[step][col_slot(tile_ref[left_at]), 5],
                             pay_recv[step][col_slot(tile_ref[right_at]), 5])
            coarse = jnp.concatenate([tile.reshape(5 * CZ, 128), edge], axis=0)
            high = coarse.astype(jnp.bfloat16)
            rest = coarse - high.astype(jnp.float32)
            middle = rest.astype(jnp.bfloat16)
            low = (rest - middle.astype(jnp.float32)).astype(jnp.bfloat16)
            parts = jnp.dot(jnp.concatenate([high, middle, low], axis=0), spread[...],
                            preferred_element_type=jnp.float32)
            count = 6 * CZ
            fine = parts[0:count] + (parts[count:2 * count] + parts[2 * count:])
            own_phase = jnp.full((5 * CZ, NM), phase_ref[sp], jnp.int32)
            plane = jnp.where(own_phase == 0, fine[0:5 * CZ, 0:NM], fine[0:5 * CZ, NM:])
            plane = plane.reshape(5, CZ, NM)
            for k in range(5):
                star[step, k, 0, :, NP:] = plane[k]
            tail = fine[5 * CZ:, :]
            left_phase = jnp.full((CZ, NM), phase_ref[left_at], jnp.int32)
            right_phase = jnp.full((CZ, NM), phase_ref[right_at], jnp.int32)
            left = jnp.where(left_phase == 0, tail[:, 0:NM], tail[:, NM:])
            right = jnp.where(right_phase == 0, tail[:, 0:NM], tail[:, NM:])
            zrecv[step, 0, Z_UP.index(11), 0, :, NP:] = left[0:1]
            zrecv[step, 1, Z_DOWN.index(13), 0, :, NP:] = right[1:2]

    def outlet(step):
        @pl.when(st == STREAM - 1)
        def _():
            for k in range(5, 10):
                star[step, k, CX + 1, :, NP:] = star[step, k, CX, :, NP:]
            for way, pop in ((0, Z_UP.index(14)), (1, Z_DOWN.index(12))):
                zrecv[step, way, pop, CX + 1, :, NP:] = zrecv[step, way, pop, CX, :, NP:]

    for load in loads:
        load.wait()

    def first(x, carry):
        collide_planes(load_input, store_star(0), x)
        return carry

    lax.fori_loop(0, CX, first, 0)

    @pl.when(st == 0)
    def _():
        pl.semaphore_wait(barrier, 5 + ROWS + COLS - 2)

    @pl.when(st != 0)
    def _():
        pl.semaphore_wait(barrier, 8)

    @pl.when(st == STREAM - 1)
    def _():
        for b in (sp_up, sp, sp_down):
            pl.semaphore_signal(ready_sem, inc=1, device_id=(st_up, b), device_id_type=MESH)

    last = STREAM - 1

    def main_start(step, way):
        @pl.when(st != (last if way == 0 else 0))
        def _():
            x_copy(step, way, 1).start()

    def main_arrive(step, way):
        @pl.when(st != (0 if way == 0 else last))
        def _():
            x_copy(step, way, 1).wait_recv()

    def main_sent(step, way):
        @pl.when(st != (last if way == 0 else 0))
        def _():
            x_copy(step, way, 1).wait_send()

    def start(*copies):
        for copy in copies:
            copy.start()

    def arrive(*copies):
        for copy in copies:
            copy.wait_recv()

    rows_start(0)

    @pl.when(st != 0)
    def _():
        start(corner_copy(0, 1), corner_copy(0, 2), x_copy(0, 1, 0))

    start(z_copy(0, 0), z_copy(0, 1), x_copy(0, 0, 0), corner_copy(0, 0), corner_copy(0, 3))

    main_start(0, 1)
    main_start(0, 0)

    wall = jnp.broadcast_to(wall_ref[...].astype(jnp.float32), (CZ, NM))
    fine_id = lax.broadcasted_iota(jnp.int32, (NM, NP), 0)
    coarse_id = lax.broadcasted_iota(jnp.int32, (NM, NP), 1)
    pick = jnp.where(lax.shift_right_logical(fine_id, 1) == coarse_id, 1.0, 0.0)
    merged = jnp.dot(wall, pick, preferred_element_type=jnp.float32)
    coarse_wall = jnp.where(merged > 0.5, 1.0, 0.0)
    solid = jnp.concatenate([coarse_wall, wall], axis=1)
    lane_id = lax.broadcasted_iota(jnp.int32, (CZ, LANES), 1)
    masks[0] = solid
    masks[1] = jnp.where((lane_id == 0) | (lane_id == NP), 1.0, pltpu.roll(solid, 1, 1))
    masks[2] = jnp.where((lane_id == NP - 1) | (lane_id == LANES - 1), 1.0,
                         pltpu.roll(solid, LANES - 1, 1))

    @pl.when(st == 0)
    def _():
        coarse_row = lax.broadcasted_iota(jnp.int32, (NP, NM), 0)
        fine_col = lax.broadcasted_iota(jnp.int32, (NP, NM), 1)
        for phase in range(2):
            place = fine_col + phase
            lower = lax.shift_right_arithmetic(place - 1, 1)
            upper = jnp.where((place & 1) == 0, 0.75, 0.25)
            low = jnp.clip(lower, 0, NP - 1)
            high = jnp.clip(lower + 1, 0, NP - 1)
            spread[:, phase * NM:(phase + 1) * NM] = (
                jnp.where(coarse_row == low, 1.0 - upper, 0.0)
                + jnp.where(coarse_row == high, upper, 0.0)).astype(jnp.bfloat16)

    def inside(plane):
        def inner(x, carry):
            plane(x)
            return carry
        lax.fori_loop(1, CX - 1, inner, 0)

    @pl.when(st == 0)
    def _():
        arrive(z_copy(0, 0), z_copy(0, 1), corner_copy(0, 1), corner_copy(0, 2), x_copy(0, 1, 0))
        advance(CX - 1, PRE)
        rows_start(1)
        start(x_copy(1, 0, 0))
        inside(advance)
        main_arrive(0, 1)
        advance(CX - 1, MAIN)
        main_start(1, 0)
        start(corner_copy(1, 0), corner_copy(1, 3))
        quads_start(0)
        pl.semaphore_wait(ready_sem, 3)
        start(corner_copy(0, 1), corner_copy(0, 2), x_copy(0, 1, 0))
        arrive(x_copy(0, 0, 0), corner_copy(0, 0), corner_copy(0, 3))
        inlet(0)
        advance(0)
        start(z_copy(1, 0), z_copy(1, 1), corner_copy(1, 1), corner_copy(1, 2), x_copy(1, 1, 0))
        quads_start(1)

    @pl.when(st != 0)
    def _():
        arrive(z_copy(0, 0), z_copy(0, 1))
        inside(advance)
        arrive(x_copy(0, 0, 0), corner_copy(0, 0), corner_copy(0, 3))
        main_arrive(0, 0)
        advance(0)
        start(x_copy(1, 1, 0), corner_copy(1, 1), corner_copy(1, 2))
        main_start(1, 1)
        arrive(x_copy(0, 1, 0), corner_copy(0, 1), corner_copy(0, 2))
        main_arrive(0, 1)
        outlet(0)
        advance(CX - 1)
        start(x_copy(1, 0, 0), corner_copy(1, 0), corner_copy(1, 3))
        main_start(1, 0)
        start(z_copy(1, 0), z_copy(1, 1))

    arrive(z_copy(1, 0), z_copy(1, 1))
    inside(finish)
    arrive(corner_copy(1, 1), corner_copy(1, 2), x_copy(1, 1, 0))
    main_arrive(1, 1)
    outlet(1)
    finish(CX - 1)
    arrive(x_copy(1, 0, 0), corner_copy(1, 0), corner_copy(1, 3))
    main_arrive(1, 0)
    inlet(1)
    finish(0)

    for step in range(2):
        for way in range(2):
            z_copy(step, way).wait_send()
            x_copy(step, way, 0).wait_send()
            main_sent(step, way)
        for which in range(4):
            corner_copy(step, which).wait_send()

    @pl.when(st == 0)
    def _():
        for step in range(2):
            for d in range(1, ROWS):
                row_copy(step, d).wait_send()
            for e in range(1, COLS):
                quad_copy(step, e).wait_send()


def put(pre_in, main_in, pre_out, main_out, sem):
    copies = [pltpu.make_async_copy(pre_in, pre_out, sem.at[0]),
              pltpu.make_async_copy(main_in, main_out, sem.at[1])]
    for copy in copies:
        copy.start()
    for copy in copies:
        copy.wait()


def local(pre_pops, main_pops, tile_map, layer_phase, wall_flags):
    vmem = pl.BlockSpec(memory_space=pltpu.VMEM)
    hbm = pl.BlockSpec(memory_space=pltpu.HBM)
    dma = pltpu.SemaphoreType.DMA
    f32 = jnp.float32
    outs = pl.pallas_call(
        body,
        out_shape=(jax.ShapeDtypeStruct(pre_pops.shape, f32),
                   jax.ShapeDtypeStruct(main_pops.shape, f32)),
        in_specs=[hbm] * 5,
        out_specs=(vmem, vmem),
        scratch_shapes=[
            pltpu.SMEM((SPAN,), jnp.int32),
            pltpu.SMEM((SPAN,), jnp.int32),
            pltpu.VMEM((1, NM), jnp.int32),
            pltpu.VMEM((19, CX, CZ, NP), f32),
            pltpu.VMEM((19, CX, CZ, NM), f32),
            pltpu.VMEM((2, 19, CX + 2, CZ, LANES), f32),
            pltpu.VMEM((2, 2, 5, CX, 1, LANES), f32),
            pltpu.VMEM((2, 2, 5, CX + 2, 1, LANES), f32),
            pltpu.VMEM((19, CZ, LANES), f32),
            pltpu.VMEM((3, CZ, LANES), f32),
            pltpu.VMEM((NP, 2 * NM), jnp.bfloat16),
            pltpu.VMEM((ROWS, 5, CZ, NP), f32),
            pltpu.VMEM((ROWS, 5, CZ, NP), f32),
            pltpu.VMEM((2, COLS, 6, CZ, NP), f32),
            pltpu.VMEM((COLS, 6, CZ, NP), f32),
            pltpu.VMEM((COLS, 6, CZ, NP), f32),
            dma((2, 2, 2)), dma((2, 2, 2)), dma((2, 2)), dma((2, 2)),
            dma((2, 4)), dma((2, 4)),
            dma((2, ROWS)), dma((2, ROWS)), dma((2, COLS)), dma((2, COLS)), dma((5,)), pltpu.SemaphoreType.REGULAR,
        ],
        compiler_params=pltpu.CompilerParams(
            collective_id=0, has_side_effects=True, vmem_limit_bytes=20 * 1024 * 1024),
    )(*[pltpu.with_memory_space_constraint(array, pltpu.HBM) for array in (
        tile_map, layer_phase, wall_flags.reshape(1, NM), pre_pops, main_pops)])
    return pl.pallas_call(
        put,
        out_shape=(jax.ShapeDtypeStruct(pre_pops.shape, f32),
                   jax.ShapeDtypeStruct(main_pops.shape, f32)),
        in_specs=[vmem] * 2,
        out_specs=(hbm, hbm),
        scratch_shapes=[dma((2,))],
        compiler_params=pltpu.CompilerParams(vmem_limit_bytes=1024 * 1024),
    )(*outs)


def solution(mesh):
    spec = jax.sharding.PartitionSpec
    blocks = spec(None, "stream", "span", None)
    return jax.shard_map(
        local,
        mesh=mesh,
        in_specs=(blocks, blocks, spec(), spec(), spec()),
        out_specs=(blocks, blocks),
        check_vma=False,
    )
```

```python
import jax
import jax.numpy as jnp
from jax import lax
from jax.experimental import pallas as pl
from jax.experimental.pallas import tpu as pltpu

VELOCITIES = (
    (0, 0, 0),
    (1, 0, 0), (-1, 0, 0), (0, 1, 0), (0, -1, 0), (0, 0, 1), (0, 0, -1),
    (1, 1, 0), (-1, -1, 0), (1, -1, 0), (-1, 1, 0),
    (1, 0, 1), (-1, 0, -1), (1, 0, -1), (-1, 0, 1),
    (0, 1, 1), (0, -1, -1), (0, 1, -1), (0, -1, 1),
)
OPPOSITE = (0, 2, 1, 4, 3, 6, 5, 8, 7, 10, 9, 12, 11, 14, 13, 16, 15, 18, 17)
ORDER = (1, 7, 9, 11, 13, 2, 8, 10, 12, 14, 0, 3, 4, 5, 6, 15, 16, 17, 18)
POS = tuple(ORDER.index(i) for i in range(19))
Z_UP = (5, 11, 14, 15, 18)
Z_DOWN = (6, 12, 13, 16, 17)
PAIRS = ((1, 2), (3, 4), (5, 6), (7, 8), (9, 10), (11, 12), (13, 14), (15, 16), (17, 18))
CX, CZ = 8, 8
NP, NM = 128, 256
LANES = NP + NM
STREAM, SPAN = 16, 32
ROWS, COLS = 8, 4
MESH = pl.DeviceIdType.MESH


def collide_planes(load, store, x, chunks=(0, 1, 2)):
    for lane in chunks:
        g = [load(i, x, lane) for i in range(19)]
        diff = {a: g[a] - g[b] for a, b in PAIRS}
        both = {a: g[a] + g[b] for a, b in PAIRS}
        axes = both[1] + both[3] + both[5]
        edges = (both[7] + both[9]) + (both[11] + both[13]) + (both[15] + both[17])
        density = (1.0 / 3.0) * g[0] + (1.0 / 18.0) * axes + (1.0 / 36.0) * edges
        mx = (1.0 / 18.0) * diff[1] + (1.0 / 36.0) * ((diff[7] + diff[9]) + (diff[11] + diff[13]))
        my = (1.0 / 18.0) * diff[3] + (1.0 / 36.0) * ((diff[7] - diff[9]) + (diff[15] + diff[17]))
        mz = (1.0 / 18.0) * diff[5] + (1.0 / 36.0) * ((diff[11] - diff[13]) + (diff[15] - diff[17]))
        inverse = 1.0 / density
        base = 1.25 * density - (1.875 * inverse) * (mx * mx + my * my + mz * mz)
        scale = 5.625 * inverse
        store(0, x, lane, base - 0.25 * g[0])
        moment = (mx, my, mz)
        for a, b in PAIRS:
            along = None
            for axis in range(3):
                c = VELOCITIES[a][axis]
                if c:
                    term = moment[axis]
                    if along is None:
                        along = term
                    else:
                        along = along + term if c > 0 else along - term
            even = base + scale * (along * along)
            odd = 3.75 * along
            store(a, x, lane, (even + odd) - 0.25 * g[a])
            store(b, x, lane, (even - odd) - 0.25 * g[b])


def body(tile_hbm, phase_hbm, wall_hbm, pre_hbm, main_hbm, pre_out, main_out,
         tile_ref, phase_ref, wall_ref, pre_ref, main_ref, star, zsend, zrecv, temp, masks, spread, rows_a, rows_b, pay_send, pay_a, pay_b,
         xs_sem, xr_sem, zs_sem, zr_sem, cs_sem, cr_sem, ys_sem, yr_sem, qs_sem, qr_sem, in_sem, ready_sem):
    rows_buf, pay_recv = (rows_a, rows_b), (pay_a, pay_b)
    st = lax.axis_index("stream")
    sp = lax.axis_index("span")
    st_up, st_down = lax.rem(st + 1, STREAM), lax.rem(st + STREAM - 1, STREAM)
    sp_up, sp_down = lax.rem(sp + 1, SPAN), lax.rem(sp + SPAN - 1, SPAN)
    row, col = lax.div(sp, COLS), lax.rem(sp, COLS)

    barrier = pltpu.get_barrier_semaphore()
    for a, b in ((st, sp_up), (st, sp_down), (st_down, sp_up), (st_down, sp), (st_down, sp_down)):
        pl.semaphore_signal(barrier, inc=1, device_id=(a, b), device_id_type=MESH)

    @pl.when(st < STREAM - 2)
    def _():
        for b in (sp_up, sp, sp_down):
            pl.semaphore_signal(barrier, inc=1, device_id=(st_up, b), device_id_type=MESH)

    @pl.when(st == 0)
    def _():
        for d in range(1, ROWS):
            peer = lax.rem(row + d, ROWS) * COLS + col
            pl.semaphore_signal(barrier, inc=1, device_id=(st, peer), device_id_type=MESH)
        for e in range(1, COLS):
            peer = row * COLS + lax.rem(col + e, COLS)
            pl.semaphore_signal(barrier, inc=1, device_id=(st, peer), device_id_type=MESH)

    loads = [pltpu.make_async_copy(source, target, in_sem.at[at])
             for at, (source, target) in enumerate((
                 (pre_hbm, pre_ref), (main_hbm, main_ref), (wall_hbm, wall_ref),
                 (tile_hbm, tile_ref), (phase_hbm, phase_ref)))]
    for load in loads:
        load.start()

    def remote(src, dst, send, recv, device):
        return pltpu.make_async_remote_copy(
            src_ref=src, dst_ref=dst, send_sem=send, recv_sem=recv,
            device_id=device, device_id_type=MESH)

    PRE, MAIN = slice(0, NP), slice(NP, LANES)

    def x_copy(step, way, part):
        cut = (PRE, MAIN)[part]
        if way == 0:
            return remote(star.at[step, 0:5, CX, :, cut], star.at[step, 0:5, 0, :, cut],
                          xs_sem.at[step, 0, part], xr_sem.at[step, 0, part], (st_up, sp))
        return remote(star.at[step, 5:10, 1, :, cut], star.at[step, 5:10, CX + 1, :, cut],
                      xs_sem.at[step, 1, part], xr_sem.at[step, 1, part], (st_down, sp))

    def z_copy(step, way):
        return remote(zsend.at[step, way], zrecv.at[step, way, :, 1:CX + 1],
                      zs_sem.at[step, way], zr_sem.at[step, way],
                      (st, sp_up if way == 0 else sp_down))

    def corner_copy(step, which):
        way, pop, x, slot, device = (
            (0, Z_UP.index(11), CX - 1, 0, (st_up, sp_up)),
            (0, Z_UP.index(14), 0, CX + 1, (st_down, sp_up)),
            (1, Z_DOWN.index(12), 0, CX + 1, (st_down, sp_down)),
            (1, Z_DOWN.index(13), CX - 1, 0, (st_up, sp_down)),
        )[which]
        return remote(zsend.at[step, way, pop, x], zrecv.at[step, way, pop, slot],
                      cs_sem.at[step, which], cr_sem.at[step, which], device)

    def row_copy(step, d):
        peer = lax.rem(row + d, ROWS) * COLS + col
        return remote(star.at[step, 0:5, CX, :, 0:NP], rows_buf[step].at[d],
                      ys_sem.at[step, d], yr_sem.at[step, d], (st, peer))

    def quad_copy(step, e):
        peer = row * COLS + lax.rem(col + e, COLS)
        return remote(pay_send.at[step, e], pay_recv[step].at[e],
                      qs_sem.at[step, e], qr_sem.at[step, e], (st, peer))

    def lanes(lane):
        return slice(lane * 128, lane * 128 + 128)

    def load_input(i, x, lane):
        if lane == 0:
            return pre_ref[i, x]
        return main_ref[i, x, :, lanes(lane - 1)]

    def load_temp(i, x, lane):
        return temp[i, :, lanes(lane)]

    def store_star(step):
        def store(i, x, lane, value):
            star[step, POS[i], x + 1, :, lanes(lane)] = value
            if i in Z_UP:
                zsend[step, 0, Z_UP.index(i), x, :, lanes(lane)] = value[CZ - 1:CZ, :]
            if i in Z_DOWN:
                zsend[step, 1, Z_DOWN.index(i), x, :, lanes(lane)] = value[0:1, :]
        return store

    def stream_plane(step, x, cut, write):
        width = cut.stop - cut.start
        row_id = lax.broadcasted_iota(jnp.int32, (CZ, width), 0)
        for i in range(19):
            cx, cy, cz = VELOCITIES[i]
            source = star[step, POS[i], x + 1 - cx, :, cut]
            if cz == 1:
                edge = zrecv[step, 0, Z_UP.index(i), x + 1 - cx, :, cut]
                source = jnp.where(row_id == 0, jnp.broadcast_to(edge, (CZ, width)),
                                   pltpu.roll(source, 1, 0))
            elif cz == -1:
                edge = zrecv[step, 1, Z_DOWN.index(i), x + 1 - cx, :, cut]
                source = jnp.where(row_id == CZ - 1, jnp.broadcast_to(edge, (CZ, width)),
                                   pltpu.roll(source, CZ - 1, 0))
            if cy == 1:
                source = pltpu.roll(source, 1, 1)
            elif cy == -1:
                source = pltpu.roll(source, width - 1, 1)
            bounced = star[step, POS[OPPOSITE[i]], x + 1, :, cut]
            write(i, jnp.where(masks[cy % 3, :, cut] > 0.5, bounced, source))

    def advance(x, cut=slice(0, LANES)):
        def write(i, value):
            temp[i, :, cut] = value
        stream_plane(0, x, cut, write)
        collide_planes(load_temp, store_star(1), x, range(cut.start // 128, cut.stop // 128))

    def finish(x):
        def write(i, value):
            pre_out[i, x] = value[:, 0:NP]
            main_out[i, x] = value[:, NP:]
        stream_plane(1, x, slice(0, LANES), write)

    def rows_start(step):
        @pl.when(st == 0)
        def _():
            for d in (4, 3, 5, 2, 6, 1, 7):
                row_copy(step, d).start()
            rows_buf[step][0] = star[step, 0:5, CX, :, 0:NP]

    small_row = lax.broadcasted_iota(jnp.int32, (CZ, 128), 0)

    def row_slot(tile):
        return lax.rem(row - lax.div(tile, COLS) + ROWS, ROWS)

    def col_slot(tile):
        return lax.rem(col - lax.rem(tile, COLS) + COLS, COLS)

    def quads_start(step):
        @pl.when(st == 0)
        def _():
            for d in range(1, ROWS):
                row_copy(step, d).wait_recv()
            for e in range(COLS):
                target = row * COLS + lax.rem(col + e, COLS)
                own = tile_ref[target]
                left = tile_ref[lax.rem(target + SPAN - 1, SPAN)]
                right = tile_ref[lax.rem(target + 1, SPAN)]
                out = pay_recv[step].at[0] if e == 0 else pay_send.at[step, e]
                out[0:5] = rows_buf[step][row_slot(own)]
                out[5] = jnp.where(
                    small_row == 0,
                    pltpu.roll(rows_buf[step][row_slot(left), 3], 1, 0),
                    pltpu.roll(rows_buf[step][row_slot(right), 4], 1, 0))
                if e:
                    quad_copy(step, e).start()

    def inlet(step):
        @pl.when(st == 0)
        def _():
            for e in range(1, COLS):
                quad_copy(step, e).wait_recv()
            left_at = lax.rem(sp + SPAN - 1, SPAN)
            right_at = lax.rem(sp + 1, SPAN)
            tile = pay_recv[step][col_slot(tile_ref[sp]), 0:5]
            edge = jnp.where(small_row == 0,
                             pay_recv[step][col_slot(tile_ref[left_at]), 5],
                             pay_recv[step][col_slot(tile_ref[right_at]), 5])
            coarse = jnp.concatenate([tile.reshape(5 * CZ, 128), edge], axis=0)
            high = coarse.astype(jnp.bfloat16)
            rest = coarse - high.astype(jnp.float32)
            middle = rest.astype(jnp.bfloat16)
            low = (rest - middle.astype(jnp.float32)).astype(jnp.bfloat16)
            parts = jnp.dot(jnp.concatenate([high, middle, low], axis=0), spread[...],
                            preferred_element_type=jnp.float32)
            count = 6 * CZ
            fine = parts[0:count] + (parts[count:2 * count] + parts[2 * count:])
            own_phase = jnp.full((5 * CZ, NM), phase_ref[sp], jnp.int32)
            plane = jnp.where(own_phase == 0, fine[0:5 * CZ, 0:NM], fine[0:5 * CZ, NM:])
            plane = plane.reshape(5, CZ, NM)
            for k in range(5):
                star[step, k, 0, :, NP:] = plane[k]
            tail = fine[5 * CZ:, :]
            left_phase = jnp.full((CZ, NM), phase_ref[left_at], jnp.int32)
            right_phase = jnp.full((CZ, NM), phase_ref[right_at], jnp.int32)
            left = jnp.where(left_phase == 0, tail[:, 0:NM], tail[:, NM:])
            right = jnp.where(right_phase == 0, tail[:, 0:NM], tail[:, NM:])
            zrecv[step, 0, Z_UP.index(11), 0, :, NP:] = left[0:1]
            zrecv[step, 1, Z_DOWN.index(13), 0, :, NP:] = right[1:2]

    def outlet(step):
        @pl.when(st == STREAM - 1)
        def _():
            for k in range(5, 10):
                star[step, k, CX + 1, :, NP:] = star[step, k, CX, :, NP:]
            for way, pop in ((0, Z_UP.index(14)), (1, Z_DOWN.index(12))):
                zrecv[step, way, pop, CX + 1, :, NP:] = zrecv[step, way, pop, CX, :, NP:]

    for load in loads:
        load.wait()

    def first(x, carry):
        collide_planes(load_input, store_star(0), x)
        return carry

    lax.fori_loop(0, CX, first, 0)

    @pl.when(st == 0)
    def _():
        pl.semaphore_wait(barrier, 5 + ROWS + COLS - 2)

    @pl.when((st > 0) & (st < STREAM - 1))
    def _():
        pl.semaphore_wait(barrier, 8)

    @pl.when(st == STREAM - 1)
    def _():
        pl.semaphore_wait(barrier, 5)

    @pl.when(st >= STREAM - 2)
    def _():
        for b in (sp_up, sp, sp_down):
            pl.semaphore_signal(ready_sem, inc=1, device_id=(st_up, b), device_id_type=MESH)

    last = STREAM - 1

    def main_start(step, way):
        @pl.when(st != (last if way == 0 else 0))
        def _():
            x_copy(step, way, 1).start()

    def main_arrive(step, way):
        @pl.when(st != (0 if way == 0 else last))
        def _():
            x_copy(step, way, 1).wait_recv()

    def main_sent(step, way):
        @pl.when(st != (last if way == 0 else 0))
        def _():
            x_copy(step, way, 1).wait_send()

    def start(*copies):
        for copy in copies:
            copy.start()

    def arrive(*copies):
        for copy in copies:
            copy.wait_recv()

    rows_start(0)

    @pl.when((st > 0) & (st < last))
    def _():
        start(corner_copy(0, 1), corner_copy(0, 2), x_copy(0, 1, 0))

    start(z_copy(0, 0), z_copy(0, 1), x_copy(0, 0, 0), corner_copy(0, 0), corner_copy(0, 3))

    @pl.when((st > 0) & (st < last))
    def _():
        x_copy(0, 1, 1).start()

    main_start(0, 0)

    wall = jnp.broadcast_to(wall_ref[...].astype(jnp.float32), (CZ, NM))
    fine_id = lax.broadcasted_iota(jnp.int32, (NM, NP), 0)
    coarse_id = lax.broadcasted_iota(jnp.int32, (NM, NP), 1)
    pick = jnp.where(lax.shift_right_logical(fine_id, 1) == coarse_id, 1.0, 0.0)
    merged = jnp.dot(wall, pick, preferred_element_type=jnp.float32)
    coarse_wall = jnp.where(merged > 0.5, 1.0, 0.0)
    solid = jnp.concatenate([coarse_wall, wall], axis=1)
    lane_id = lax.broadcasted_iota(jnp.int32, (CZ, LANES), 1)
    masks[0] = solid
    masks[1] = jnp.where((lane_id == 0) | (lane_id == NP), 1.0, pltpu.roll(solid, 1, 1))
    masks[2] = jnp.where((lane_id == NP - 1) | (lane_id == LANES - 1), 1.0,
                         pltpu.roll(solid, LANES - 1, 1))

    @pl.when(st == 0)
    def _():
        coarse_row = lax.broadcasted_iota(jnp.int32, (NP, NM), 0)
        fine_col = lax.broadcasted_iota(jnp.int32, (NP, NM), 1)
        for phase in range(2):
            place = fine_col + phase
            lower = lax.shift_right_arithmetic(place - 1, 1)
            upper = jnp.where((place & 1) == 0, 0.75, 0.25)
            low = jnp.clip(lower, 0, NP - 1)
            high = jnp.clip(lower + 1, 0, NP - 1)
            spread[:, phase * NM:(phase + 1) * NM] = (
                jnp.where(coarse_row == low, 1.0 - upper, 0.0)
                + jnp.where(coarse_row == high, upper, 0.0)).astype(jnp.bfloat16)

    def inside(plane):
        def inner(x, carry):
            plane(x)
            return carry
        lax.fori_loop(1, CX - 1, inner, 0)

    @pl.when(st == 0)
    def _():
        arrive(z_copy(0, 0), z_copy(0, 1), corner_copy(0, 1), corner_copy(0, 2), x_copy(0, 1, 0))
        advance(CX - 1, PRE)
        rows_start(1)
        start(x_copy(1, 0, 0))
        inside(advance)
        pl.semaphore_wait(ready_sem, 3)
        start(corner_copy(0, 1), corner_copy(0, 2), x_copy(0, 1, 0))
        main_arrive(0, 1)
        advance(CX - 1, MAIN)
        main_start(1, 0)
        start(corner_copy(1, 0), corner_copy(1, 3))
        quads_start(0)
        arrive(x_copy(0, 0, 0), corner_copy(0, 0), corner_copy(0, 3))
        inlet(0)
        advance(0)
        start(z_copy(1, 0), z_copy(1, 1), corner_copy(1, 1), corner_copy(1, 2), x_copy(1, 1, 0))
        quads_start(1)

    @pl.when(st != 0)
    def _():
        arrive(z_copy(0, 0), z_copy(0, 1))
        inside(advance)

        @pl.when(st == last)
        def _():
            pl.semaphore_wait(ready_sem, 3)
            start(corner_copy(0, 1), corner_copy(0, 2), x_copy(0, 1, 0), x_copy(0, 1, 1))

        arrive(x_copy(0, 1, 0), corner_copy(0, 1), corner_copy(0, 2))
        main_arrive(0, 1)
        outlet(0)
        advance(CX - 1)
        start(x_copy(1, 0, 0), corner_copy(1, 0), corner_copy(1, 3))
        main_start(1, 0)
        arrive(x_copy(0, 0, 0), corner_copy(0, 0), corner_copy(0, 3))
        main_arrive(0, 0)
        advance(0)
        start(x_copy(1, 1, 0), corner_copy(1, 1), corner_copy(1, 2))
        main_start(1, 1)
        start(z_copy(1, 0), z_copy(1, 1))

    arrive(z_copy(1, 0), z_copy(1, 1))
    inside(finish)
    arrive(corner_copy(1, 1), corner_copy(1, 2), x_copy(1, 1, 0))
    main_arrive(1, 1)
    outlet(1)
    finish(CX - 1)
    arrive(x_copy(1, 0, 0), corner_copy(1, 0), corner_copy(1, 3))
    main_arrive(1, 0)
    inlet(1)
    finish(0)

    for step in range(2):
        for way in range(2):
            z_copy(step, way).wait_send()
            x_copy(step, way, 0).wait_send()
            main_sent(step, way)
        for which in range(4):
            corner_copy(step, which).wait_send()

    @pl.when(st == 0)
    def _():
        for step in range(2):
            for d in range(1, ROWS):
                row_copy(step, d).wait_send()
            for e in range(1, COLS):
                quad_copy(step, e).wait_send()


def put(pre_in, main_in, pre_out, main_out, sem):
    copies = [pltpu.make_async_copy(pre_in, pre_out, sem.at[0]),
              pltpu.make_async_copy(main_in, main_out, sem.at[1])]
    for copy in copies:
        copy.start()
    for copy in copies:
        copy.wait()


def local(pre_pops, main_pops, tile_map, layer_phase, wall_flags):
    vmem = pl.BlockSpec(memory_space=pltpu.VMEM)
    hbm = pl.BlockSpec(memory_space=pltpu.HBM)
    dma = pltpu.SemaphoreType.DMA
    f32 = jnp.float32
    outs = pl.pallas_call(
        body,
        out_shape=(jax.ShapeDtypeStruct(pre_pops.shape, f32),
                   jax.ShapeDtypeStruct(main_pops.shape, f32)),
        in_specs=[hbm] * 5,
        out_specs=(vmem, vmem),
        scratch_shapes=[
            pltpu.SMEM((SPAN,), jnp.int32),
            pltpu.SMEM((SPAN,), jnp.int32),
            pltpu.VMEM((1, NM), jnp.int32),
            pltpu.VMEM((19, CX, CZ, NP), f32),
            pltpu.VMEM((19, CX, CZ, NM), f32),
            pltpu.VMEM((2, 19, CX + 2, CZ, LANES), f32),
            pltpu.VMEM((2, 2, 5, CX, 1, LANES), f32),
            pltpu.VMEM((2, 2, 5, CX + 2, 1, LANES), f32),
            pltpu.VMEM((19, CZ, LANES), f32),
            pltpu.VMEM((3, CZ, LANES), f32),
            pltpu.VMEM((NP, 2 * NM), jnp.bfloat16),
            pltpu.VMEM((ROWS, 5, CZ, NP), f32),
            pltpu.VMEM((ROWS, 5, CZ, NP), f32),
            pltpu.VMEM((2, COLS, 6, CZ, NP), f32),
            pltpu.VMEM((COLS, 6, CZ, NP), f32),
            pltpu.VMEM((COLS, 6, CZ, NP), f32),
            dma((2, 2, 2)), dma((2, 2, 2)), dma((2, 2)), dma((2, 2)),
            dma((2, 4)), dma((2, 4)),
            dma((2, ROWS)), dma((2, ROWS)), dma((2, COLS)), dma((2, COLS)), dma((5,)), pltpu.SemaphoreType.REGULAR,
        ],
        compiler_params=pltpu.CompilerParams(
            collective_id=0, has_side_effects=True, vmem_limit_bytes=20 * 1024 * 1024),
    )(*[pltpu.with_memory_space_constraint(array, pltpu.HBM) for array in (
        tile_map, layer_phase, wall_flags.reshape(1, NM), pre_pops, main_pops)])
    return pl.pallas_call(
        put,
        out_shape=(jax.ShapeDtypeStruct(pre_pops.shape, f32),
                   jax.ShapeDtypeStruct(main_pops.shape, f32)),
        in_specs=[vmem] * 2,
        out_specs=(hbm, hbm),
        scratch_shapes=[dma((2,))],
        compiler_params=pltpu.CompilerParams(vmem_limit_bytes=1024 * 1024),
    )(*outs)


def solution(mesh):
    spec = jax.sharding.PartitionSpec
    blocks = spec(None, "stream", "span", None)
    return jax.shard_map(
        local,
        mesh=mesh,
        in_specs=(blocks, blocks, spec(), spec(), spec()),
        out_specs=(blocks, blocks),
        check_vma=False,
    )
```
